32 devices in a mesh: px: 4 (over z), py: 8 (over y, x, core).
Axes of the slice: x: 2, y: 2, z: 4, core: 2. Of those that a mesh axis runs over, the one named last changes fastest.
Arguments:
- current_state: float32 [5, 125, 32768], P(None, None, ('px', 'py')), may hold values from -6 to 6
- state_old: float32 [5, 125, 32768], P(None, None, ('px', 'py')), may hold values from -6 to 6
- jacobian: float32 [32768], P(('px', 'py')), may hold values from 0.5 to 2
- volume_operator_list: float32 [3, 125, 125], replicated, may hold values from -0.3125 to 0.3125
- flux_jacobian_list: float32 [3, 5, 5], replicated, may hold values from -2.5 to 2.5
- penalty: float32 [5], replicated, may hold values from 0.5 to 2
- cut_owner: int32 [1280, 1], P(('px', 'py')), may hold values from 0 to 7; in each aligned block of 40 rows (0 to 39, 40 to 79, ...) at most 8 rows name the same one
- cut_element: int32 [1280], P(('px', 'py')), may hold values from 0 to 1023
- cut_mass: float32 [1280, 125, 125], P(('px', 'py')), may hold values from -0.5 to 0.5
- cut_operator: float32 [1280, 125, 125], P(('px', 'py')), may hold values from -0.5 to 0.5
- body_holder_index: int32 [24], P('px'), may hold values from 0 to 7
- body_points: float32 [192, 3, 128], P(('px', 'py')), may hold values from -1 to 1
- body_normals: float32 [192, 3, 128], P(('px', 'py')), may hold values from -6 to 6
- body_weights: float32 [192, 128], P(('px', 'py')), may hold values from 0.01 to 0.1
- covered: int32 [192, 16], P(('px', 'py')), may hold values from 0 to 1023
Outputs:
- residual: float32 [5, 125, 32768], P(None, None, ('px', 'py'))
The draws below stay inside these ranges and needn't reach their ends.
Inputs may be any that keep to these rules, and one draw needn't show every extreme that they name: `cut_owner`: among the 40 rows of one device no owner is named by more than 8 rows, a bound that some block reaches. Owners are py indices within the same slab. `cut_element`: several cut blocks may belong to one element; their terms add. `body_holder_index`: only the slot of the owning device is read for each body. `covered`: an element may be listed more than once; its terms add.
All inputs are finite; a program needn't handle non-finite values.
Results may differ from the reference program's by a relative error of at most 0.0001.
Values sent between devices are 32-bit elements; how exact they have to be, the bound alone decides.
No kernel may reach another device: no remote copies, remote signals or barrier semaphores. Data moves between devices by JAX's collectives and lax.ppermute only.
A program may use at most 128 MiB of HBM per device.

```python
import math
import jax
import jax.numpy as jnp
import numpy as np
from jax import lax

DEGREE = 4
MODES = 125
FACE = 25
NVAR = 5
ELEM_DEV = 1024
LAYERS = 8
COLS = 128
ELEMS = 32768
CUT_DEV = 40
CUTS = 1280
CAP = 8
BODIES = 6
OWNERS = 24
BODY_SLOTS = 192
QPTS = 128
COVERED = 16
N_PX = 4
N_PY = 8


def plant(entries, own_key, smallest, largest):
    longest = entries.shape.index(max(entries.shape))
    spots = []
    for shift in (0, 1):
        where = [jax.random.randint(jax.random.fold_in(own_key, axis), (), 0, length) for axis, length in enumerate(entries.shape)]
        where[longest] = (where[longest] + shift) % entries.shape[longest]
        spots.append(tuple(where))
    return entries.at[spots[0]].set(smallest).at[spots[1]].set(largest)


def level_of(stream_key, dims, split, low, top_value):
    loudness = 1.0
    for dim, shards_of in split:
        heights = jax.random.uniform(jax.random.fold_in(jax.random.fold_in(stream_key, 6), dim), (shards_of,), jnp.float32, low / len(split), top_value / len(split))
        loudness = loudness * jnp.repeat(jnp.exp(heights), dims[dim] // shards_of).reshape((-1,) + (1,) * (len(dims) - 1 - dim))
    return loudness


def shared_out(stream_key, own, number, rows, amount, top, limit, slope):
    ranking = jax.random.permutation(stream_key, amount)
    packed, usual = load_shares(amount, rows * top, limit, slope, True), load_shares(amount, rows * top, limit, slope, False)
    places = jnp.arange(amount)

    def named(sizes, offset_by):
        used = int((sizes > 0).sum())
        fixed = max(1, used // 4)
        moved = fixed + (places - fixed + offset_by * (used - fixed)) % max(1, amount - fixed)
        return jnp.zeros((amount,), jnp.int32).at[ranking[jnp.where(places < fixed, places, moved)]].set(jnp.asarray(sizes, jnp.int32))

    sizes = jnp.where(number % 4 == 0, named(packed, number // 4), named(usual, number - number // 4 - 1))
    mixed = jax.random.permutation(jax.random.fold_in(own, 3), amount)
    giver, receiver = mixed[0:amount // 2 * 2:2], mixed[1:amount // 2 * 2:2]
    room = jnp.minimum(sizes[giver] - 1, limit - sizes[receiver]) // 2
    room = jnp.where((giver == ranking[0]) | (receiver == ranking[0]) | (sizes[receiver] == 0), 0, jnp.maximum(room, 0))
    moved = jax.random.randint(jax.random.fold_in(own, 4), (amount // 2,), 0, 1 << 20) % (room + 1)
    sizes = sizes.at[giver].add(-moved).at[receiver].add(moved)
    items = jnp.searchsorted(jnp.cumsum(sizes), jnp.arange(rows * top), side="right").astype(jnp.int32)
    listing = items.reshape(top, rows).T
    listing = listing[jax.random.permutation(jax.random.fold_in(own, 1), rows)]
    offset_by = jax.random.randint(jax.random.fold_in(own, 2), (rows, 1), 0, top)
    return jnp.take_along_axis(listing, (jnp.arange(top)[None, :] + offset_by) % top, axis=1)


def load_shares(count, total, reach, skew, full):
    weights = [(1 << 20) // math.isqrt(grade ** skew) + 1 for grade in range(1, count + 1)]
    largest = reach if full else min(reach, max(-(-total // count), total * weights[0] // sum(weights)))
    least = 1 if total - largest >= count - 1 else 0
    counts, spare = [largest] + [least] * (count - 1), total - largest - least * (count - 1)
    while spare > 0:
        movable = [i for i in range(1, count) if counts[i] < largest] or [i for i in range(1, count) if counts[i] < reach]
        whole, budget = sum([weights[i] for i in movable]), spare
        for i in movable:
            addition = min(reach - counts[i], max(1, budget * weights[i] // whole), spare)
            counts[i] = counts[i] + addition
            spare = spare - addition
    return np.array(counts)


def centred(key, dims, scale, most, shards=(), held_as=jnp.bfloat16):
    level = level_of(key, dims, shards, -0.22, 0.18) if shards else 1.0
    array = jax.random.normal(key, dims, jnp.float32) * scale * level
    return jnp.minimum(jnp.maximum(array, -most), most).astype(held_as)


def setup_inputs(seed: int = 0) -> dict:
    splits = jax.random.split(jax.random.key(seed), 16)
    current_state = centred(splits[0], (NVAR, MODES, ELEMS), 1.0, 6.0, ((2, 32),), jnp.float32)
    state_old = centred(splits[1], (NVAR, MODES, ELEMS), 1.0, 6.0, ((2, 32),), jnp.float32)
    jacobian = jnp.clip(jnp.exp(math.log(2.0) - 1.3862944 * jax.random.uniform(splits[2], (ELEMS,), jnp.float32) ** level_of(splits[2], (ELEMS,), ((0, 32),), -0.2, 0.2)), 0.5, 2.0)
    volume_operator_list = centred(splits[3], (3, MODES, MODES), (3 * MODES) ** -0.5, 0.3125, (), jnp.float32)
    flux_jacobian_list = centred(splits[4], (3, NVAR, NVAR), NVAR ** -0.5, 2.5, (), jnp.float32)
    penalty = jnp.clip(jnp.exp(jax.random.uniform(splits[5], (NVAR,), jnp.float32, math.log(0.5), math.log(2.0))), 0.5, 2.0)
    cut_owner_keys = jax.random.split(jax.random.fold_in(splits[6], 1), CUTS // CUT_DEV)
    cut_owner_turns = jax.random.permutation(jax.random.fold_in(splits[6], 3), CUTS // CUT_DEV)
    cut_owner = jax.vmap(lambda own, number: shared_out(jax.random.fold_in(splits[6], 2), own, number, CUT_DEV, N_PY, 1, CAP, 2))(cut_owner_keys, cut_owner_turns).reshape((CUTS, 1))
    cut_element = plant(jax.random.randint(splits[7], (CUTS,), 0, ELEM_DEV), jax.random.fold_in(splits[7], 1), 0, ELEM_DEV - 1).astype(jnp.int32)
    cut_mass = centred(splits[8], (CUTS, MODES, MODES), MODES ** -0.5, 0.5, ((0, 32),), jnp.float32)
    cut_operator = centred(splits[9], (CUTS, MODES, MODES), MODES ** -0.5, 0.5, ((0, 32),), jnp.float32)
    body_holder_index = plant(jax.random.randint(splits[10], (OWNERS,), 0, N_PY), jax.random.fold_in(splits[10], 1), 0, N_PY - 1).astype(jnp.int32)
    body_points = jnp.clip(jax.random.uniform(splits[11], (BODY_SLOTS, 3, QPTS), jnp.float32, -1.0, 1.0) * level_of(splits[11], (BODY_SLOTS, 3, QPTS), ((0, 32),), -0.4, 0.0), -1.0, 1.0)
    body_normals = centred(splits[12], (BODY_SLOTS, 3, QPTS), 1.0, 6.0, ((0, 32),), jnp.float32)
    body_weights = jnp.clip(jnp.exp(math.log(0.1) - 2.3025851 * jax.random.uniform(splits[13], (BODY_SLOTS, QPTS), jnp.float32) ** level_of(splits[13], (BODY_SLOTS, QPTS), ((0, 32),), -0.2, 0.2)), 0.01, 0.1)
    covered = plant(jax.random.randint(splits[14], (BODY_SLOTS, COVERED), 0, ELEM_DEV), jax.random.fold_in(splits[14], 1), 0, ELEM_DEV - 1).astype(jnp.int32)
    return dict(current_state=current_state, state_old=state_old, jacobian=jacobian, volume_operator_list=volume_operator_list, flux_jacobian_list=flux_jacobian_list, penalty=penalty, cut_owner=cut_owner, cut_element=cut_element, cut_mass=cut_mass, cut_operator=cut_operator, body_holder_index=body_holder_index, body_points=body_points, body_normals=body_normals, body_weights=body_weights, covered=covered)


TOP_PRECISION = lax.Precision.HIGHEST


def mode_weights():
    degree_one = DEGREE + 1
    mode_index = jnp.arange(degree_one ** 3, dtype=jnp.int32)
    degree_x = (mode_index // (degree_one * degree_one)).astype(jnp.float32)
    degree_y = ((mode_index // degree_one) % degree_one).astype(jnp.float32)
    degree_z = (mode_index % degree_one).astype(jnp.float32)
    return 8.0 / ((2.0 * degree_x + 1.0) * (2.0 * degree_y + 1.0) * (2.0 * degree_z + 1.0))


def legendre_table(coords):
    poly_table = [jnp.ones_like(coords), coords]
    for degree_now in range(1, DEGREE):
        poly_table.append(((2.0 * degree_now + 1.0) * coords * poly_table[degree_now] - degree_now * poly_table[degree_now - 1]) / (degree_now + 1.0))
    return jnp.stack(poly_table[:DEGREE + 1], axis=0)


def basis_rows(points):
    along_x = legendre_table(points[..., 0, :])
    along_y = legendre_table(points[..., 1, :])
    along_z = legendre_table(points[..., 2, :])
    basis_vals = along_x[:, None, None] * along_y[None, :, None] * along_z[None, None, :]
    leading = points.shape[:-2]
    basis_vals = basis_vals.reshape(((DEGREE + 1) ** 3,) + leading + (points.shape[-1],))
    return jnp.moveaxis(basis_vals, 0, -2)


def to_lines(traces):
    shaped = traces.reshape(NVAR, FACE, N_PX, N_PY, LAYERS, COLS).transpose(0, 1, 3, 2, 4, 5)
    return shaped.reshape(NVAR, FACE, N_PY, N_PX * LAYERS, COLS)


def from_lines(traces):
    shaped = traces.reshape(NVAR, FACE, N_PY, N_PX, LAYERS, COLS).transpose(0, 1, 3, 2, 4, 5)
    return shaped.reshape(NVAR, FACE, ELEMS)


def reference(current_state, state_old, jacobian, volume_operator_list, flux_jacobian_list, penalty, cut_owner, cut_element, cut_mass, cut_operator, body_holder_index, body_points, body_normals, body_weights, covered):
    degree_one = DEGREE + 1
    change = current_state - state_old
    residual = mode_weights()[None, :, None] * jacobian[None, None, :] * change
    for space_direction in range(3):
        blended_state = jnp.einsum("jr,rti->jti", flux_jacobian_list[space_direction], current_state, precision=TOP_PRECISION)
        residual = residual - jnp.einsum("fz,jzx->jfx", volume_operator_list[space_direction], blended_state, precision=TOP_PRECISION)

    split_modes = current_state.reshape(NVAR, degree_one, FACE, ELEMS)
    parity = jnp.where(jnp.arange(degree_one, dtype=jnp.int32) % 2 == 0, 1.0, -1.0).astype(jnp.float32)
    upper_line = to_lines(jnp.sum(split_modes, axis=1))
    lower_line = to_lines(jnp.sum(split_modes * parity[None, :, None, None], axis=1))
    zero_layer = jnp.zeros_like(upper_line[:, :, :, :1])
    from_above = jnp.concatenate([lower_line[:, :, :, 1:], zero_layer], axis=3)
    from_below = jnp.concatenate([zero_layer, upper_line[:, :, :, :-1]], axis=3)
    jump_top = from_lines(from_above - upper_line)
    jump_bottom = from_lines(from_below - lower_line)
    face_term = penalty[:, None, None, None] * (jump_top[:, None] + parity[None, :, None, None] * jump_bottom[:, None])
    residual = residual - face_term.reshape(NVAR, MODES, ELEMS)

    slab_of = jnp.arange(CUTS, dtype=jnp.int32) // (CUT_DEV * N_PY)
    target = ((slab_of * N_PY + cut_owner[:, 0].astype(jnp.int32)) * ELEM_DEV + cut_element.astype(jnp.int32)).astype(jnp.int32)
    cut_terms = jnp.einsum("cmn,vnc->vmc", cut_mass, change[:, :, target], precision=TOP_PRECISION) - jnp.einsum("cmn,vnc->vmc", cut_operator, current_state[:, :, target], precision=TOP_PRECISION)
    residual = residual.at[:, :, target].add(cut_terms)

    owners = body_holder_index.reshape(N_PX, BODIES).astype(jnp.int32)
    points_grid = body_points.reshape(N_PX, N_PY, BODIES, 3, QPTS)
    normal_grid = body_normals.reshape(N_PX, N_PY, BODIES, 3, QPTS)
    weight_grid = body_weights.reshape(N_PX, N_PY, BODIES, QPTS)
    covered_grid = covered.reshape(N_PX, N_PY, BODIES, COVERED).astype(jnp.int32)
    slab_ids = jnp.arange(N_PX, dtype=jnp.int32)
    device_base = (slab_ids[:, None] * N_PY + jnp.arange(N_PY, dtype=jnp.int32)[None, :]) * ELEM_DEV
    for body_index in range(BODIES):
        owner_ids = owners[:, body_index]
        points = points_grid[slab_ids, owner_ids, body_index]
        normals = normal_grid[slab_ids, owner_ids, body_index]
        weights = weight_grid[slab_ids, owner_ids, body_index]
        basis_now = basis_rows(points)
        targets = (device_base[:, :, None] + covered_grid[:, :, body_index, :]).astype(jnp.int32)
        gathered = current_state[:, :, targets]
        surf_trace = jnp.einsum("smq,vmspo->vqspo", basis_now, gathered, precision=TOP_PRECISION)
        normal_x = jnp.transpose(normals[:, 0, :])[:, :, None, None]
        normal_y = jnp.transpose(normals[:, 1, :])[:, :, None, None]
        normal_z = jnp.transpose(normals[:, 2, :])[:, :, None, None]
        speed = normal_x * surf_trace[1] + normal_y * surf_trace[2] + normal_z * surf_trace[3]
        body_wall_flux = jnp.stack([speed + 0.5 * surf_trace[0], normal_x * surf_trace[4], normal_y * surf_trace[4], normal_z * surf_trace[4], 1.4 * speed], axis=0)
        weighted = body_wall_flux * jnp.transpose(weights)[None, :, :, None, None]
        lifted = jnp.einsum("smq,vqspo->vmspo", basis_now, weighted, precision=TOP_PRECISION)
        residual = residual.at[:, :, targets].add(-lifted)
    return residual
```

```python
import functools

import jax
import jax.numpy as jnp
from jax import lax
from jax.experimental import pallas as pl
from jax.experimental.pallas import tpu as pltpu
from jax.sharding import PartitionSpec as P

DEGREE = 4
LAYERS = 8
LANES = 128
SUBS = 8
MIB = 1 << 20

F32 = jnp.float32
BF16 = jnp.bfloat16
NN = (((1,), (0,)), ((), ()))
NT = (((1,), (1,)), ((), ()))


def pad8(count):
    return -(-count // SUBS) * SUBS


def iota(shape, dim):
    return lax.broadcasted_iota(jnp.int32, shape, dim)


def halves(value):
    high = value.astype(BF16)
    return high, (value - high.astype(F32)).astype(BF16)


def mxu(left, right, dims=NN):
    return lax.dot_general(left, right, dims, preferred_element_type=F32)


def product(left, right, dims=NN):
    left_high, left_low = left
    right_high, right_low = right
    return mxu(left_high, right_high, dims) + (
        mxu(left_low, right_high, dims) + mxu(left_high, right_low, dims)
    )


def exact_dot(left, right):
    return lax.dot_general(
        left, right, NN, precision=lax.Precision.HIGHEST, preferred_element_type=F32
    )


def pick_lanes(values, lanes):
    return jnp.take_along_axis(values, jnp.broadcast_to(lanes, values.shape), axis=1)


def params(limit):
    return pltpu.CompilerParams(vmem_limit_bytes=limit * MIB)


def whole(array):
    return pl.BlockSpec(array.shape, lambda *_: (0,) * array.ndim)


def smem():
    return pl.BlockSpec(memory_space=pltpu.SMEM)


def ids_kernel(cap, share, hold_ref, owner_ref, elem_ref, points_ref, normals_ref, weights_ref, out_ref, rows_ref):
    peers = out_ref.shape[0]
    bodies = points_ref.shape[0]
    cuts = owner_ref.shape[0]
    me = lax.axis_index("py")
    owner = owner_ref[...]
    named = (owner == iota((cuts, LANES), 1)).astype(F32)
    earlier = (iota((cuts, cuts), 1) < iota((cuts, cuts), 0)).astype(F32)
    place = jnp.sum(mxu(earlier, named) * named, axis=1, keepdims=True).astype(jnp.int32)
    placing = (owner * cap + place == iota((cuts, LANES), 1)).astype(F32)
    ids = exact_dot(elem_ref[...].astype(F32) + 1.0, placing) - 1.0
    rows_ref[...] = jnp.zeros_like(rows_ref)
    for body in range(bodies):
        mine = hold_ref[body] == me
        rows_ref[body * 7 : body * 7 + 3] = jnp.where(mine, points_ref[body], 0.0)
        rows_ref[body * 7 + 3 : body * 7 + 6] = jnp.where(mine, normals_ref[body], 0.0)
        rows_ref[body * 7 + 6 : body * 7 + 7] = jnp.where(mine, weights_ref[body : body + 1], 0.0)
    for peer in range(peers):
        out_ref[peer] = jnp.zeros((SUBS, LANES), F32)
        out_ref[peer, 0:1] = ids
        out_ref[peer, 1 : 1 + share] = rows_ref[peer * share : (peer + 1) * share]


def rim_kernel(state_ref, covered_ref, low_ref, up_ref, rows_ref, column_ref, lane_ref, acc_ref):
    step = pl.program_id(0)
    nvar, modes, _ = state_ref.shape
    face = modes // (DEGREE + 1)
    bodies, count = covered_ref.shape

    @pl.when(step == 0)
    def _():
        spread = (iota((count, LANES), 1) % count == iota((count, LANES), 0)).astype(F32)
        tiled = exact_dot(covered_ref[...].astype(F32), spread)
        kept = jnp.where(iota((bodies, LANES), 1) // count == iota((bodies, LANES), 0), tiled + 1.0, 0.0)
        row = jnp.sum(kept, axis=0, keepdims=True) - 1.0
        spot = jnp.broadcast_to(row, (LANES, LANES))
        column_ref[...] = spot.T.astype(jnp.int32)
        lane_ref[...] = row.astype(jnp.int32)
        acc_ref[...] = jnp.zeros_like(acc_ref)

    def sums(var):
        part = [state_ref[var, i * face : (i + 1) * face, :] for i in range(DEGREE + 1)]
        return (part[0] + part[2]) + part[4], part[1] + part[3]

    @pl.when(step == 0)
    def _():
        for var in range(nvar):
            even, odd = sums(var)
            low_ref[var] = jnp.zeros(low_ref.shape[1:], F32)
            low_ref[var, :face] = even - odd

    @pl.when(step == pl.num_programs(0) - 1)
    def _():
        for var in range(nvar):
            even, odd = sums(var)
            up_ref[var] = jnp.zeros(up_ref.shape[1:], F32)
            up_ref[var, :face] = even + odd

    spots = lane_ref[...]
    here = spots // LANES == step
    for var in range(nvar):
        found = pick_lanes(state_ref[var], spots % LANES)
        acc_ref[var, :modes] = jnp.where(here, found, acc_ref[var, :modes])

    @pl.when(step == pl.num_programs(0) - 1)
    def _():
        for var in range(nvar):
            rows_ref[var] = acc_ref[var].T


def pick_kernel(cap, share, got_ref, state_ref, old_ref, out_ref, column_ref, lane_ref, acc_ref):
    step = pl.program_id(0)
    nvar, modes, _ = state_ref.shape
    peers = got_ref.shape[0]
    half = LANES // 2
    lane = iota((1, LANES), 1)

    @pl.when(step == 0)
    def _():
        me = lax.axis_index("py")
        row = jnp.zeros((1, LANES), F32) - 1.0
        for peer in range(peers):
            moved = pltpu.roll(got_ref[peer, 0:1], ((peer - me) * cap + LANES) % LANES, 1)
            row = jnp.where(lane // cap == peer, moved, row)
        row = jnp.where(lane < half, row, pltpu.roll(row, half, 1))
        column_ref[...] = jnp.broadcast_to(row, (LANES, LANES)).T.astype(jnp.int32)
        lane_ref[...] = row.astype(jnp.int32)
        acc_ref[...] = jnp.zeros_like(acc_ref)
        data = got_ref[0]
        for peer in range(1, peers):
            data = data + got_ref[peer]
        for peer in range(peers):
            out_ref[peer, 2 * nvar, :, :] = data

    spots = lane_ref[...]
    here = (spots + LANES) // LANES == step + 1
    for var in range(nvar):
        found = jnp.where(
            lane < half,
            pick_lanes(state_ref[var], spots & (LANES - 1)),
            pick_lanes(old_ref[var], spots & (LANES - 1)),
        )
        acc_ref[var, :modes] = jnp.where(here, found, acc_ref[var, :modes])

    @pl.when(step == pl.num_programs(0) - 1)
    def _():
        for var in range(nvar):
            rows = acc_ref[var].T
            for peer in range(peers):
                for kind in range(2):
                    first = kind * half + peer * cap
                    if cap < SUBS:
                        out_ref[peer, kind * nvar + var] = jnp.zeros((SUBS, LANES), F32)
                    out_ref[peer, kind * nvar + var, :cap] = rows[first : first + cap]


def main_kernel(
    flux_ref, penalty_ref, state_ref, under_ref, over_ref, old_ref, jac_ref, below_ref, above_ref, operator_ref,
    out_ref, matrix_ref, right_ref, face_ref,
):
    step = pl.program_id(0)
    steps = pl.num_programs(0)
    nvar, modes, width = state_ref.shape
    degree_one = DEGREE + 1
    face = modes // degree_one
    size = nvar * LANES

    @pl.when(step == 0)
    def _():
        matrix_ref[...] = jnp.zeros_like(matrix_ref)
        right_ref[...] = jnp.zeros_like(right_ref)
        face_ref[...] = jnp.zeros_like(face_ref)
        row, col = iota((modes, modes), 0), iota((modes, modes), 1)
        paired = (row % face == col % face) & ((row // face + col // face) % 2 == 0)
        own_face = jnp.where(paired, 2.0, 0.0).astype(F32)
        for var in range(nvar):
            for other in range(nvar):
                block = -(flux_ref[0, var, other] * operator_ref[0])
                for direction in range(1, 3):
                    block = block - flux_ref[direction, var, other] * operator_ref[direction]
                if var == other:
                    block = block + penalty_ref[var] * own_face
                high, low = halves(block)
                rows = slice(var * LANES, var * LANES + modes)
                for place, part in ((0, high), (size, high), (2 * size, low)):
                    matrix_ref[rows, place + other * LANES : place + other * LANES + modes] = part

    for var in range(nvar):
        high, low = halves(state_ref[var])
        rows = slice(var * LANES, var * LANES + modes)
        for place, part in ((0, high), (size, low), (2 * size, high)):
            right_ref[place + var * LANES : place + var * LANES + modes] = part

    product_now = mxu(matrix_ref[...], right_ref[...])
    mode = iota((modes, width), 0)
    weight = 8.0 / (
        (2.0 * (mode // (degree_one * degree_one)).astype(F32) + 1.0)
        * (2.0 * (mode // degree_one % degree_one).astype(F32) + 1.0)
        * (2.0 * (mode % degree_one).astype(F32) + 1.0)
    )
    scale = weight * jac_ref[...]

    def sums(ref, var):
        part = [ref[var, i * face : (i + 1) * face, :] for i in range(degree_one)]
        return (part[0] + part[2]) + part[4], part[1] + part[3]

    for var in range(nvar):
        even, odd = sums(state_ref, var)
        upper, lower = even + odd, even - odd
        even, odd = sums(over_ref, var)
        above = jnp.where(step == steps - 1, above_ref[var, :face], even - odd)
        even, odd = sums(under_ref, var)
        below = jnp.where(step == 0, below_ref[var, :face], even + odd)
        above = jnp.concatenate([lower[:, LANES:], above], axis=1)
        below = jnp.concatenate([below, upper[:, : width - LANES]], axis=1)
        plus = penalty_ref[var] * (above + below)
        minus = penalty_ref[var] * (above - below)
        for i in range(degree_one):
            face_ref[i * face : (i + 1) * face] = minus if i % 2 else plus
        change = state_ref[var] - old_ref[var]
        out_ref[var] = (
            product_now[var * LANES : var * LANES + modes] + scale * change
        ) - face_ref[:modes]


def cut_kernel(owner_ref, got_ref, mass_ref, operator_ref, out_ref, seen_ref, columns_ref):
    step = pl.program_id(0)
    block, modes, _ = mass_ref.shape
    peers, nvar = out_ref.shape[0], out_ref.shape[1]

    @pl.when(step == 0)
    def _():
        out_ref[...] = jnp.zeros_like(out_ref)
        for peer in range(peers):
            seen_ref[peer] = 0

    lane = iota((modes, LANES), 1)
    columns = jnp.zeros((modes, LANES), F32)
    spots = []
    for index in range(block):
        owner = owner_ref[step * block + index]
        place = seen_ref[owner]
        seen_ref[owner] = place + 1
        spots.append((owner, place))
        for var in range(nvar):
            state = got_ref[owner, var, pl.ds(place, 1), :]
            change = state - got_ref[owner, nvar + var, pl.ds(place, 1), :]
            term = mass_ref[index] * change[:, :modes] - operator_ref[index] * state[:, :modes]
            total = jnp.sum(term, axis=1, keepdims=True)
            columns = jnp.where(lane == index * nvar + var, total, columns)
    columns_ref[...] = jnp.zeros_like(columns_ref)
    columns_ref[:modes] = columns
    rows = columns_ref[...].T
    for index, (owner, place) in enumerate(spots):
        for var in range(nvar):
            first = index * nvar + var
            out_ref[owner, var, pl.ds(place, 1), :] = rows[first : first + 1]


def body_kernel(bodies, count, share, got_ref, rows_ref, column_ref, base_ref, out_ref, data_ref, lift_ref, left_ref):
    step = pl.program_id(0)
    peers = got_ref.shape[0]
    nvar, modes, width = out_ref.shape
    degree_one = DEGREE + 1

    @pl.when(step == 0)
    def _():
        for peer in range(peers):
            data_ref[peer * share : (peer + 1) * share] = got_ref[peer, 0, 1 : 1 + share]
        lift_ref[...] = jnp.zeros_like(lift_ref)
        mode, degree = iota((LANES, SUBS), 0), iota((LANES, SUBS), 1)
        real = mode < modes
        spreads = []
        for digit in (mode // (degree_one * degree_one), mode // degree_one % degree_one, mode % degree_one):
            chosen = (real & (digit == degree)).astype(BF16)
            spreads.append(jnp.concatenate([chosen, chosen, chosen], axis=1))
        ones = jnp.ones((1, LANES), F32)
        none = jnp.zeros((SUBS - degree_one, LANES), F32)
        for body in range(bodies):
            basis = None
            for axis in range(3):
                coords = data_ref[body * 7 + axis : body * 7 + axis + 1]
                table = [ones, coords]
                for n in range(1, DEGREE):
                    table.append(((2.0 * n + 1.0) * coords * table[n] - n * table[n - 1]) / (n + 1.0))
                stacked = jnp.concatenate(table + [none], axis=0)
                high = stacked.astype(BF16)
                rest = stacked - high.astype(F32)
                middle, low = halves(rest)
                factor = mxu(spreads[axis], jnp.concatenate([high, middle, low], axis=0))
                basis = factor if basis is None else basis * factor
            basis = halves(basis)
            rows = jnp.concatenate(
                [rows_ref[var, body * count : (body + 1) * count] for var in range(nvar)], axis=0
            )
            trace = product(halves(rows), basis)
            trace = [trace[var * count : (var + 1) * count] for var in range(nvar)]
            normal = [data_ref[body * 7 + 3 + axis : body * 7 + 4 + axis] for axis in range(3)]
            weights = data_ref[body * 7 + 6 : body * 7 + 7]
            speed = normal[0] * trace[1] + normal[1] * trace[2] + normal[2] * trace[3]
            flux = [speed + 0.5 * trace[0]] + [normal[axis] * trace[4] for axis in range(3)] + [1.4 * speed]
            weighted = jnp.concatenate([part * weights for part in flux], axis=0)
            lifted = product(halves(weighted), basis, NT)
            for var in range(nvar):
                lift_ref[var, body * count : (body + 1) * count] = lifted[var * count : (var + 1) * count]
        for var in range(nvar):
            high, low = halves(lift_ref[var].T)
            left_ref[var * LANES : (var + 1) * LANES, :LANES] = high
            left_ref[var * LANES : (var + 1) * LANES, LANES:] = low

    spots = jnp.concatenate([column_ref[...]] * (width // LANES), axis=1)
    chosen = (spots == iota((LANES, width), 1) + step * width).astype(BF16)
    added = mxu(left_ref[...], jnp.concatenate([chosen, chosen], axis=0))
    for var in range(nvar):
        out_ref[var] = base_ref[var] - added[var * LANES : var * LANES + modes]


def last_kernel(cap, got_ref, column_ref, base_ref, out_ref, slots_ref, left_ref):
    step = pl.program_id(0)
    peers = got_ref.shape[0]
    nvar, modes, width = out_ref.shape
    half = LANES // 2

    @pl.when(step == 0)
    def _():
        slots_ref[...] = jnp.zeros_like(slots_ref)
        for var in range(nvar):
            for peer in range(peers):
                slots_ref[peer * cap : (peer + 1) * cap] = got_ref[peer, var, :cap]
            high, low = halves(slots_ref[...].T)
            left_ref[var * LANES : (var + 1) * LANES, :half] = high[:, :half]
            left_ref[var * LANES : (var + 1) * LANES, half:] = low[:, :half]

    spots = jnp.concatenate([column_ref[...]] * (width // LANES), axis=1)
    chosen = (spots == iota((LANES, width), 1) + step * width).astype(BF16)
    added = mxu(left_ref[...], chosen)
    for var in range(nvar):
        out_ref[var] = base_ref[var] + added[var * LANES : var * LANES + modes]


def shift(value, axis, step):
    count = lax.axis_size(axis)
    pairs = [(source, source + step) for source in range(count) if 0 <= source + step < count]
    return lax.ppermute(value, axis, pairs)


def exchange(value):
    return lax.all_to_all(value, "py", split_axis=0, concat_axis=0, tiled=True)


def local(
    current_state, state_old, jacobian, volume_operator_list, flux_jacobian_list, penalty, cut_owner, cut_element,
    cut_mass, cut_operator, body_holder_index, body_points, body_normals, body_weights, covered,
):
    nvar, modes, elems = current_state.shape
    columns = elems // LAYERS
    face = modes // (DEGREE + 1)
    peers = lax.axis_size("py")
    cuts = cut_owner.shape[0]
    bodies, count = covered.shape
    cap = max(2, cuts * 3 // (2 * peers) + 1)
    share = -(-bodies * 7 // peers)
    half = LANES // 2
    assert columns == LANES and peers * cap <= half and bodies * count <= LANES
    assert cap <= SUBS and 1 + share <= SUBS and modes <= LANES
    shaped = jax.ShapeDtypeStruct
    wide = 2 * LANES
    steps = elems // wide
    layer = pl.BlockSpec((nvar, modes, LANES), lambda step: (0, 0, step))
    chunk = pl.BlockSpec((nvar, modes, wide), lambda step: (0, 0, step))

    asked = pl.pallas_call(
        functools.partial(ids_kernel, cap, share),
        out_shape=shaped((peers, SUBS, LANES), F32),
        in_specs=[smem()] + [pl.BlockSpec(memory_space=pltpu.VMEM)] * 5,
        out_specs=pl.BlockSpec(memory_space=pltpu.VMEM),
        scratch_shapes=[pltpu.VMEM((pad8(peers * share), LANES), F32)],
        compiler_params=params(8),
        name="ids",
    )(body_holder_index, cut_owner, cut_element.reshape(1, cuts), body_points, body_normals, body_weights)
    requests = exchange(asked)

    face_rows = shaped((nvar, pad8(face), LANES), F32)
    square = shaped((LANES, LANES), jnp.int32)
    stack = shaped((nvar, LANES, LANES), F32)
    lower, upper, covered_rows, covered_column = pl.pallas_call(
        rim_kernel,
        grid=(LAYERS,),
        out_shape=(face_rows, face_rows, stack, square),
        in_specs=[layer, whole(covered)],
        out_specs=(whole(face_rows), whole(face_rows), whole(stack), whole(square)),
        scratch_shapes=[pltpu.VMEM((1, LANES), jnp.int32), pltpu.VMEM(stack.shape, F32)],
        compiler_params=params(8),
        name="rim",
    )(current_state, covered)
    above_rim = shift(lower, "px", -1)
    below_rim = shift(upper, "px", 1)

    reply = shaped((peers, 2 * nvar + 1, SUBS, LANES), F32)
    states_out, slot_column = pl.pallas_call(
        functools.partial(pick_kernel, cap, share),
        grid=(LAYERS,),
        out_shape=(reply, square),
        in_specs=[whole(requests), layer, layer],
        out_specs=(whole(reply), whole(square)),
        scratch_shapes=[pltpu.VMEM((1, LANES), jnp.int32), pltpu.VMEM(stack.shape, F32)],
        compiler_params=params(8),
        name="pick",
    )(requests, current_state, state_old)
    replies = exchange(states_out)

    out = shaped(current_state.shape, F32)
    size = nvar * LANES
    residual = pl.pallas_call(
        main_kernel,
        grid=(steps,),
        out_shape=out,
        in_specs=[
            smem(),
            smem(),
            chunk,
            pl.BlockSpec((nvar, modes, LANES), lambda step: (0, 0, jnp.maximum(2 * step - 1, 0))),
            pl.BlockSpec((nvar, modes, LANES), lambda step: (0, 0, jnp.minimum(2 * step + 2, LAYERS - 1))),
            chunk,
            pl.BlockSpec((1, wide), lambda step: (0, step)),
            whole(below_rim),
            whole(above_rim),
            whole(volume_operator_list),
        ],
        out_specs=chunk,
        scratch_shapes=[
            pltpu.VMEM((size, 3 * size), BF16),
            pltpu.VMEM((3 * size, wide), BF16),
            pltpu.VMEM((LANES, wide), F32),
        ],
        compiler_params=params(24),
        cost_estimate=pl.CostEstimate(
            flops=6 * size * size * elems, transcendentals=0, bytes_accessed=4 * 4 * nvar * modes * elems
        ),
        name="main",
    )(
        flux_jacobian_list, penalty, current_state, current_state, current_state, state_old,
        jacobian.reshape(1, elems), below_rim, above_rim, volume_operator_list,
    )

    group = next(size for size in (8, 10, 5, 4, 2, 1) if cuts % size == 0)
    terms = shaped((peers, nvar, SUBS, LANES), F32)
    blocks = pl.BlockSpec((group, modes, modes), lambda step: (step, 0, 0))
    results_out = pl.pallas_call(
        cut_kernel,
        grid=(cuts // group,),
        out_shape=terms,
        in_specs=[smem(), whole(replies), blocks, blocks],
        out_specs=whole(terms),
        scratch_shapes=[pltpu.SMEM((peers,), jnp.int32), pltpu.VMEM((LANES, LANES), F32)],
        compiler_params=params(12),
        name="cut",
    )(cut_owner.reshape(cuts), replies, cut_mass, cut_operator)
    results = exchange(results_out)

    residual = pl.pallas_call(
        functools.partial(body_kernel, bodies, count, share),
        grid=(steps,),
        out_shape=out,
        in_specs=[
            pl.BlockSpec((peers, 1, SUBS, LANES), lambda step: (0, 2 * nvar, 0, 0)),
            whole(covered_rows),
            whole(covered_column),
            chunk,
        ],
        out_specs=chunk,
        scratch_shapes=[
            pltpu.VMEM((pad8(peers * share), LANES), F32),
            pltpu.VMEM(stack.shape, F32),
            pltpu.VMEM((size, wide), BF16),
        ],
        input_output_aliases={3: 0},
        compiler_params=params(12),
        name="body",
    )(replies, covered_rows, covered_column, residual)

    return pl.pallas_call(
        functools.partial(last_kernel, cap),
        grid=(steps,),
        out_shape=out,
        in_specs=[whole(results), whole(slot_column), chunk],
        out_specs=chunk,
        scratch_shapes=[pltpu.VMEM((LANES, LANES), F32), pltpu.VMEM((size, LANES), BF16)],
        input_output_aliases={2: 0},
        compiler_params=params(12),
        name="last",
    )(results, slot_column, residual)


def solution(mesh):
    both = ("px", "py")
    in_specs = (
        P(None, None, both),
        P(None, None, both),
        P(both),
        P(),
        P(),
        P(),
        P(both, None),
        P(both),
        P(both, None, None),
        P(both, None, None),
        P("px"),
        P(both, None, None),
        P(both, None, None),
        P(both, None),
        P(both, None),
    )
    return jax.shard_map(
        local, mesh=mesh, in_specs=in_specs, out_specs=P(None, None, both), check_vma=False
    )
```

```python
import functools

import jax
import jax.numpy as jnp
from jax import lax
from jax.experimental import pallas as pl
from jax.experimental.pallas import tpu as pltpu
from jax.sharding import PartitionSpec as P

DEGREE = 4
LAYERS = 8
LANES = 128
SUBS = 8
MIB = 1 << 20

F32 = jnp.float32
BF16 = jnp.bfloat16
NN = (((1,), (0,)), ((), ()))
NT = (((1,), (1,)), ((), ()))


def pad8(count):
    return -(-count // SUBS) * SUBS


def iota(shape, dim):
    return lax.broadcasted_iota(jnp.int32, shape, dim)


def halves(value):
    high = value.astype(BF16)
    return high, (value - high.astype(F32)).astype(BF16)


def mxu(left, right, dims=NN):
    return lax.dot_general(left, right, dims, preferred_element_type=F32)


def product(left, right, dims=NN):
    left_high, left_low = left
    right_high, right_low = right
    return mxu(left_high, right_high, dims) + (
        mxu(left_low, right_high, dims) + mxu(left_high, right_low, dims)
    )


def exact_dot(left, right, dims=NN):
    return lax.dot_general(
        left, right, dims, precision=lax.Precision.HIGHEST, preferred_element_type=F32
    )


def pick_lanes(values, lanes):
    return jnp.take_along_axis(values, jnp.broadcast_to(lanes, values.shape), axis=1)


def params(limit):
    return pltpu.CompilerParams(vmem_limit_bytes=limit * MIB)


def kept():
    return pl.BlockSpec(memory_space=pltpu.VMEM)


def scalars():
    return pl.BlockSpec(memory_space=pltpu.SMEM)


def remote():
    return pl.BlockSpec(memory_space=pl.ANY)


def in_hbm(array):
    return pltpu.with_memory_space_constraint(array, pltpu.HBM)


def in_vmem(array):
    return pltpu.with_memory_space_constraint(array, pltpu.VMEM)


def stored(array):
    return pltpu.HBM(array.shape, array.dtype)


def whole(array):
    return pl.BlockSpec(array.shape, lambda *_: (0,) * len(array.shape))


def trace_sums(ref, var, first, width):
    face = ref.shape[1] // (DEGREE + 1)
    part = [ref[var, i * face : (i + 1) * face, first : first + width] for i in range(DEGREE + 1)]
    even, odd = (part[0] + part[2]) + part[4], part[1] + part[3]
    return even + odd, even - odd


def ids_kernel(cap, share, hold_ref, owner_ref, elem_ref, points_ref, normals_ref, weights_ref, out_ref, rows_ref):
    peers = out_ref.shape[0]
    bodies = points_ref.shape[0]
    cuts = owner_ref.shape[1]
    me = lax.axis_index("py")
    owner = owner_ref[...]
    named = (owner == iota((pad8(peers), cuts), 0)).astype(F32)
    earlier = (iota((cuts, cuts), 0) < iota((cuts, cuts), 1)).astype(F32)
    place = jnp.sum(mxu(named, earlier) * named, axis=0, keepdims=True).astype(jnp.int32)
    compact = (owner * cap + place == iota((LANES, cuts), 0)).astype(F32)
    ids = exact_dot(elem_ref[...].astype(F32) + 1.0, compact, NT) - 1.0
    rows_ref[...] = jnp.zeros_like(rows_ref)
    for body in range(bodies):
        mine = hold_ref[body] == me
        rows_ref[body * 7 : body * 7 + 3] = jnp.where(mine, points_ref[body], 0.0)
        rows_ref[body * 7 + 3 : body * 7 + 6] = jnp.where(mine, normals_ref[body], 0.0)
        rows_ref[body * 7 + 6 : body * 7 + 7] = jnp.where(mine, weights_ref[body : body + 1], 0.0)
    for peer in range(peers):
        out_ref[peer] = jnp.zeros((SUBS, LANES), F32)
        out_ref[peer, 0:1] = ids
        out_ref[peer, 1 : 1 + share] = rows_ref[peer * share : (peer + 1) * share]


def load_kernel(covered_ref, state_hbm, state_ref, first_ref, second_ref, rows_ref, column_ref, acc_ref, sems):
    even = lax.axis_index("px") % 2 == 0
    nvar, modes, elems = state_ref.shape
    face = modes // (DEGREE + 1)
    bodies, count = covered_ref.shape
    copies = [pltpu.make_async_copy(state_hbm.at[var], state_ref.at[var], sems.at[var]) for var in range(nvar)]
    for copy in copies:
        copy.start()

    spread = (iota((count, LANES), 1) % count == iota((count, LANES), 0)).astype(F32)
    tiled = exact_dot(covered_ref[...].astype(F32), spread)
    mine = iota((bodies, LANES), 1) // count == iota((bodies, LANES), 0)
    row = jnp.sum(jnp.where(mine, tiled + 1.0, 0.0), axis=0, keepdims=True) - 1.0
    column_ref[...] = jnp.broadcast_to(row, (LANES, LANES)).T.astype(jnp.int32)
    spots = row.astype(jnp.int32)
    acc_ref[...] = jnp.zeros_like(acc_ref)
    first_ref[...] = jnp.zeros_like(first_ref)
    second_ref[...] = jnp.zeros_like(second_ref)
    for var in range(nvar):
        copies[var].wait()
        lower = trace_sums(state_ref, var, 0, LANES)[1]
        upper = trace_sums(state_ref, var, elems - LANES, LANES)[0]
        first_ref[var, :face] = jnp.where(even, upper, lower)
        second_ref[var, :face] = jnp.where(even, lower, upper)
        found = acc_ref[var, :modes]
        for layer in range(elems // LANES):
            lanes = slice(layer * LANES, (layer + 1) * LANES)
            picked = pick_lanes(state_ref[var, :, lanes], spots & (LANES - 1))
            found = jnp.where((spots + LANES) // LANES == layer + 1, picked, found)
        acc_ref[var, :modes] = found
        rows_ref[var] = acc_ref[var].T


def pick_kernel(cap, share, got_ref, state_ref, old_hbm, out_ref, column_ref, old_ref, acc_ref, sems):
    nvar, modes, elems = state_ref.shape
    peers = got_ref.shape[0]
    half = LANES // 2
    copies = [pltpu.make_async_copy(old_hbm.at[var], old_ref.at[var], sems.at[var]) for var in range(nvar)]
    for copy in copies:
        copy.start()
    lane = iota((1, LANES), 1)
    me = lax.axis_index("py")
    row = jnp.zeros((1, LANES), F32) - 1.0
    for peer in range(peers):
        moved = pltpu.roll(got_ref[peer, 0:1], ((peer - me) * cap + LANES) % LANES, 1)
        row = jnp.where(lane // cap == peer, moved, row)
    row = jnp.where(lane < half, row, pltpu.roll(row, half, 1))
    spots = row.astype(jnp.int32)
    acc_ref[...] = jnp.zeros_like(acc_ref)

    def gather(ref, var, wanted):
        found = acc_ref[var, :modes]
        for layer in range(elems // LANES):
            picked = pick_lanes(ref[var, :, layer * LANES : (layer + 1) * LANES], spots & (LANES - 1))
            found = jnp.where(wanted & ((spots + LANES) // LANES == layer + 1), picked, found)
        acc_ref[var, :modes] = found

    for var in range(nvar):
        gather(state_ref, var, lane < half)
    data = got_ref[0]
    for peer in range(1, peers):
        data = data + got_ref[peer]
    for peer in range(peers):
        out_ref[peer, 2 * nvar, :, :] = data
    column = jnp.broadcast_to(row, (LANES, LANES)).T.astype(jnp.int32)
    if cap < SUBS:
        column_ref[...] = jnp.zeros_like(column_ref) - 1
    for peer in range(peers):
        column_ref[peer * SUBS : peer * SUBS + cap] = column[peer * cap : (peer + 1) * cap]
    for var in range(nvar):
        copies[var].wait()
        gather(old_ref, var, lane >= half)
        rows = acc_ref[var].T
        for peer in range(peers):
            for kind in range(2):
                first = kind * half + peer * cap
                if cap < SUBS:
                    out_ref[peer, kind * nvar + var] = jnp.zeros((SUBS, LANES), F32)
                out_ref[peer, kind * nvar + var, :cap] = rows[first : first + cap]


def main_kernel(
    flux_ref, penalty_ref, jac_ref, operator_hbm, state_hbm, old_hbm, _,
    out_ref, _unused, state_ref, old_ref, operator_ref, padded_ref, matrix_ref, right_ref, product_ref, face_ref, sems,
):
    nvar, modes, elems = state_ref.shape
    degree_one = DEGREE + 1
    face = modes // degree_one
    size = nvar * LANES
    width = face_ref.shape[2]
    copies = [
        pltpu.make_async_copy(source, target, sems.at[index])
        for index, (source, target) in enumerate(
            ((operator_hbm, operator_ref), (state_hbm, state_ref), (old_hbm, old_ref))
        )
    ]
    copies[0].start()
    copies[1].start()
    padded_ref[...] = jnp.zeros_like(padded_ref)
    gap = LANES - modes
    for var in range(nvar):
        for place in (0, size):
            last = place + var * LANES + modes
            right_ref[:, last : last + gap] = jnp.zeros((right_ref.shape[0], gap, width), BF16)

    def digits(index):
        high = jnp.floor((index + 0.5) * (1.0 / face))
        return high, index - face * high

    row_high, row_low = digits(iota((LANES, LANES), 0).astype(F32))
    col_high, col_low = digits(iota((LANES, LANES), 1).astype(F32))
    apart = row_high - col_high
    apart = apart - 2.0 * jnp.floor(0.5 * apart)
    inside = iota((LANES, LANES), 0) < modes
    own_face = jnp.where((row_low == col_low) & (apart == 0.0) & inside, 2.0, 0.0)
    own_face = jnp.where(iota((LANES, LANES), 1) < modes, own_face, 0.0)
    copies[0].wait()
    copies[2].start()
    padded_ref[:, :modes, :modes] = operator_ref[...]
    for var in range(nvar):
        for other in range(nvar):
            block = -(flux_ref[var, 0, other] * padded_ref[0])
            for direction in range(1, 3):
                block = block - flux_ref[var, direction, other] * padded_ref[direction]
            if var == other:
                block = block + penalty_ref[var] * own_face
            high, low = halves(block)
            rows = slice(var * LANES, (var + 1) * LANES)
            for place, part in ((0, high), (size, high), (2 * size, low)):
                matrix_ref[rows, place + other * LANES : place + (other + 1) * LANES] = part
    mid = jnp.floor((row_low + 0.5) * (1.0 / degree_one))
    weight = 8.0 / (
        (2.0 * row_high + 1.0) * (2.0 * mid + 1.0) * (2.0 * (row_low - degree_one * mid) + 1.0)
    )
    weight = jnp.concatenate([weight] * (width // LANES), axis=1)[:modes]

    def split(chunk):
        for var in range(nvar):
            high, low = halves(state_ref[var, :, chunk * width : (chunk + 1) * width])
            for place, part in ((0, high), (size, low)):
                right_ref[chunk % 2, place + var * LANES : place + var * LANES + modes] = part

    def multiply(chunk):
        product_ref[chunk % 2] = mxu(matrix_ref[:, : 2 * size], right_ref[chunk % 2]) + mxu(
            matrix_ref[:, 2 * size :], right_ref[chunk % 2, :size]
        )

    copies[1].wait()
    split(0)
    multiply(0)
    split(1)
    copies[2].wait()
    below = [jnp.zeros((face, LANES), F32)] * nvar
    chunks = elems // width
    for chunk in range(chunks):
        first = chunk * width
        lanes = slice(first, first + width)
        if chunk + 1 < chunks:
            multiply(chunk + 1)
        if chunk + 2 < chunks:
            split(chunk + 2)
        scale = weight * jac_ref[:, lanes]
        for var in range(nvar):
            upper, lower = trace_sums(state_ref, var, first, width)
            if chunk + 1 < chunks:
                above = trace_sums(state_ref, var, first + width, LANES)[1]
            else:
                above = jnp.zeros((face, LANES), F32)
            above = jnp.concatenate([lower[:, LANES:], above], axis=1)
            under = jnp.concatenate([below[var], upper[:, : width - LANES]], axis=1)
            below[var] = upper[:, width - LANES :]
            plus = penalty_ref[var] * (above + under)
            minus = penalty_ref[var] * (above - under)
            for i in range(degree_one):
                face_ref[var, i * face : (i + 1) * face] = minus if i % 2 else plus
            change = state_ref[var, :, lanes] - old_ref[var, :, lanes]
            out_ref[var, :, lanes] = (
                product_ref[chunk % 2, var * LANES : var * LANES + modes] + scale * change
            ) - face_ref[var, :modes]


def cut_kernel(owner_ref, got_ref, mass_hbm, operator_hbm, _, out_ref, mass_ref, operator_ref, left_ref, term_ref, spot_ref, seen_ref, sems):
    groups, modes = mass_ref.shape[:2]
    peers, nvar = out_ref.shape[0], out_ref.shape[1]
    kinds = got_ref.shape[1]
    copies = []
    for group in range(groups):
        rows = slice(group * SUBS, (group + 1) * SUBS)
        copies.append(
            (
                pltpu.make_async_copy(mass_hbm.at[:, rows], mass_ref.at[group], sems.at[0, group]),
                pltpu.make_async_copy(operator_hbm.at[:, rows], operator_ref.at[group], sems.at[1, group]),
            )
        )
        for copy in copies[-1]:
            copy.start()
    out_ref[...] = jnp.zeros_like(out_ref)
    for peer in range(peers):
        seen_ref[peer] = 0
    got = got_ref.reshape(peers * kinds * SUBS, LANES)
    out = out_ref.reshape(peers * nvar * SUBS, LANES)
    for index in range(groups * SUBS):
        owner = owner_ref[index]
        place = seen_ref[owner]
        seen_ref[owner] = place + 1
        spot_ref[index] = owner * (nvar * SUBS) + place
        first = owner * (kinds * SUBS) + place
        states = got[pl.ds(first, nvar, stride=SUBS), :]
        changes = states - got[pl.ds(first + nvar * SUBS, nvar, stride=SUBS), :]
        for kind, value in enumerate((changes, -states)):
            high = value.astype(BF16).astype(F32)
            left_ref[index, 2 * SUBS * kind : 2 * SUBS * kind + nvar] = high
            left_ref[index, 2 * SUBS * kind + SUBS : 2 * SUBS * kind + SUBS + nvar] = value - high
    for group in range(groups):
        for copy in copies[group]:
            copy.wait()
        for inner in range(SUBS):
            index = group * SUBS + inner
            total = None
            for kind, ref in enumerate((mass_ref, operator_ref)):
                block = ref.at[group].reshape(modes * SUBS, modes)[pl.ds(inner, modes, stride=SUBS), :]
                left = left_ref[index, 2 * SUBS * kind : 2 * SUBS * (kind + 1), :modes].astype(BF16)
                for right in halves(block):
                    term = mxu(left, right, NT)
                    total = term if total is None else total + term
            term_ref[index, :, :modes] = total[:SUBS] + total[SUBS:]
    for index in range(groups * SUBS):
        out[pl.ds(spot_ref[index], nvar, stride=SUBS), :modes] = term_ref[index, :nvar, :modes]


def body_kernel(bodies, count, share, got_ref, rows_ref, column_ref, base_ref, out_ref, data_ref, basis_ref, lift_ref, left_ref):
    peers = got_ref.shape[0]
    nvar, modes, elems = out_ref.shape
    degree_one = DEGREE + 1
    for peer in range(peers):
        data_ref[peer * share : (peer + 1) * share] = got_ref[peer, 2 * nvar, 1 : 1 + share]
    lift_ref[...] = jnp.zeros_like(lift_ref)
    mode, degree = iota((LANES, SUBS), 0), iota((LANES, SUBS), 1)
    real = mode < modes
    spreads = []
    for digit in (mode // (degree_one * degree_one), mode // degree_one % degree_one, mode % degree_one):
        chosen = (real & (digit == degree)).astype(BF16)
        spreads.append(jnp.concatenate([chosen, chosen, chosen], axis=1))
    ones = jnp.ones((1, LANES), F32)
    none = jnp.zeros((SUBS - degree_one, LANES), F32)
    for body in range(bodies):
        basis = None
        for axis in range(3):
            coords = data_ref[body * 7 + axis : body * 7 + axis + 1]
            table = [ones, coords]
            for n in range(1, DEGREE):
                table.append(((2.0 * n + 1.0) * coords * table[n] - n * table[n - 1]) / (n + 1.0))
            stacked = jnp.concatenate(table + [none], axis=0)
            high = stacked.astype(BF16)
            middle, low = halves(stacked - high.astype(F32))
            factor = mxu(spreads[axis], jnp.concatenate([high, middle, low], axis=0))
            basis = factor if basis is None else basis * factor
        basis_ref[0, body], basis_ref[1, body] = halves(basis)
    bases = [(basis_ref[0, body], basis_ref[1, body]) for body in range(bodies)]
    traces = []
    for body in range(bodies):
        rows = jnp.concatenate([rows_ref[var, body * count : (body + 1) * count] for var in range(nvar)], axis=0)
        traces.append(product(halves(rows), bases[body]))
    fluxes = []
    for body in range(bodies):
        trace = [traces[body][var * count : (var + 1) * count] for var in range(nvar)]
        normal = [data_ref[body * 7 + 3 + axis : body * 7 + 4 + axis] for axis in range(3)]
        weights = data_ref[body * 7 + 6 : body * 7 + 7]
        speed = normal[0] * trace[1] + normal[1] * trace[2] + normal[2] * trace[3]
        flux = [speed + 0.5 * trace[0]] + [normal[axis] * trace[4] for axis in range(3)] + [1.4 * speed]
        fluxes.append(halves(jnp.concatenate([part * weights for part in flux], axis=0)))
    for body in range(bodies):
        lifted = product(fluxes[body], bases[body], NT)
        for var in range(nvar):
            lift_ref[var, body * count : (body + 1) * count] = lifted[var * count : (var + 1) * count]
    for var in range(nvar):
        high, low = halves(lift_ref[var].T)
        left_ref[var * LANES : (var + 1) * LANES, :LANES] = high
        left_ref[var * LANES : (var + 1) * LANES, LANES:] = low

    width = 2 * LANES
    spots = jnp.concatenate([column_ref[...]] * (width // LANES), axis=1)
    for first in range(0, elems, width):
        chosen = (spots == iota((LANES, width), 1) + first).astype(BF16)
        added = mxu(left_ref[...], jnp.concatenate([chosen, chosen], axis=0))
        for var in range(nvar):
            lanes = slice(first, first + width)
            out_ref[var, :, lanes] = base_ref[var, :, lanes] - added[var * LANES : var * LANES + modes]


def last_kernel(penalty_ref, got_ref, column_ref, first_ref, second_ref, base_ref, out_hbm, out_ref, left_ref, face_ref, sems):
    nvar, modes, elems = out_ref.shape
    slots = column_ref.shape[0]
    degree_one = DEGREE + 1
    face = modes // degree_one
    width = 2 * LANES
    even = lax.axis_index("px") % 2 == 0
    for var in range(nvar):
        rows = got_ref[:, var].reshape(slots, LANES).T
        left_ref[var * LANES : (var + 1) * LANES] = jnp.concatenate(halves(rows), axis=1)
        first, second = first_ref[var, :face], second_ref[var, :face]
        above = penalty_ref[var] * jnp.where(even, first, second)
        below = penalty_ref[var] * jnp.where(even, second, first)
        for i in range(degree_one):
            face_ref[0, var, i * face : (i + 1) * face] = -below if i % 2 else below
            face_ref[1, var, i * face : (i + 1) * face] = above

    spots = jnp.concatenate([column_ref[...]] * (width // LANES), axis=1)
    copies = []
    for start in range(0, elems, width):
        lanes = slice(start, start + width)
        chosen = (spots == iota((slots, width), 1) + start).astype(BF16)
        chosen = jnp.concatenate([chosen, chosen], axis=0)
        for var in range(nvar):
            added = mxu(left_ref[var * LANES : (var + 1) * LANES], chosen)[:modes]
            total = base_ref[var, :, lanes] + added
            if start == 0:
                total = jnp.concatenate([total[:, :LANES] - face_ref[0, var, :modes], total[:, LANES:]], axis=1)
            if start + width == elems:
                total = jnp.concatenate([total[:, :LANES], total[:, LANES:] - face_ref[1, var, :modes]], axis=1)
            out_ref[var, :, lanes] = total
            copies.append(
                pltpu.make_async_copy(out_ref.at[var, :, lanes], out_hbm.at[var, :, lanes], sems.at[len(copies)])
            )
            copies[-1].start()
    for copy in copies:
        copy.wait()


def swap(value, axis, odd):
    count = lax.axis_size(axis)
    pairs = [(low, low + 1) for low in range(odd, count - 1, 2)]
    return lax.ppermute(value, axis, pairs + [(high, low) for low, high in pairs])


def exchange(value):
    return lax.all_to_all(value, "py", split_axis=0, concat_axis=0, tiled=True)


def local(
    current_state, state_old, jacobian, volume_operator_list, flux_jacobian_list, penalty, cut_owner, cut_element,
    cut_mass, cut_operator, body_holder_index, body_points, body_normals, body_weights, covered,
):
    nvar, modes, elems = current_state.shape
    columns = elems // LAYERS
    face = modes // (DEGREE + 1)
    peers = lax.axis_size("py")
    cuts = cut_owner.shape[0]
    bodies, count = covered.shape
    cap = max(2, cuts * 3 // (2 * peers) + 1)
    share = -(-bodies * 7 // peers)
    half = LANES // 2
    slots = peers * SUBS
    assert columns == LANES and peers * cap <= half and bodies * count <= LANES
    assert cap <= SUBS and 1 + share <= SUBS and modes <= LANES and cuts % SUBS == 0
    shaped = jax.ShapeDtypeStruct
    wide = 2 * LANES
    size = nvar * LANES

    owner_row = in_hbm(cut_owner.reshape(1, cuts))
    small = [in_hbm(array) for array in (cut_element.reshape(1, cuts), body_points, body_normals, body_weights)]
    asked = shaped((peers, SUBS, LANES), F32)
    asked = pl.pallas_call(
        functools.partial(ids_kernel, cap, share),
        grid=(1,),
        out_shape=asked,
        in_specs=[scalars(), whole(owner_row)] + [whole(array) for array in small],
        out_specs=whole(asked),
        scratch_shapes=[pltpu.VMEM((pad8(peers * share), LANES), F32)],
        compiler_params=params(4),
        name="ids",
    )(in_hbm(body_holder_index), owner_row, *small)
    requests = exchange(asked)

    field = pltpu.VMEM(current_state.shape, F32)
    face_rows = shaped((nvar, pad8(face), LANES), F32)
    stack = shaped((nvar, LANES, LANES), F32)
    square = shaped((LANES, LANES), jnp.int32)
    scratch = pltpu.VMEM(stack.shape, F32)
    state, first_rim, second_rim, covered_rows, covered_column = pl.pallas_call(
        load_kernel,
        grid=(1,),
        out_shape=(field, face_rows, stored(face_rows), stored(stack), stored(square)),
        in_specs=[whole(covered), remote()],
        out_specs=(kept(), whole(face_rows), whole(face_rows), whole(stack), whole(square)),
        scratch_shapes=[scratch, pltpu.SemaphoreType.DMA((nvar,))],
        compiler_params=params(4),
        name="load",
    )(in_hbm(covered), in_hbm(current_state))
    first_rim = swap(first_rim, "px", 0)

    reply = shaped((peers, 2 * nvar + 1, SUBS, LANES), F32)
    column = shaped((slots, LANES), jnp.int32)
    states_out, slot_column = pl.pallas_call(
        functools.partial(pick_kernel, cap, share),
        grid=(1,),
        out_shape=(reply, stored(column)),
        in_specs=[kept(), kept(), remote()],
        out_specs=(whole(reply), whole(column)),
        scratch_shapes=[pltpu.VMEM(current_state.shape, F32), scratch, pltpu.SemaphoreType.DMA((nvar,))],
        compiler_params=params(6),
        name="pick",
    )(requests, in_vmem(state), in_hbm(state_old))
    replies = exchange(states_out)

    jacobian_row = in_hbm(jacobian.reshape(1, elems))
    residual, second_rim = pl.pallas_call(
        main_kernel,
        grid=(1,),
        out_shape=(field, stored(face_rows)),
        in_specs=[scalars(), scalars(), whole(jacobian_row)] + [remote()] * 4,
        out_specs=(kept(), remote()),
        scratch_shapes=[
            pltpu.VMEM(current_state.shape, F32),
            pltpu.VMEM(current_state.shape, F32),
            pltpu.VMEM(volume_operator_list.shape, F32),
            pltpu.VMEM((3, LANES, LANES), F32),
            pltpu.VMEM((size, 3 * size), BF16),
            pltpu.VMEM((2, 2 * size, wide), BF16),
            pltpu.VMEM((2, size, wide), F32),
            pltpu.VMEM((nvar, LANES, wide), F32),
            pltpu.SemaphoreType.DMA((3,)),
        ],
        input_output_aliases={6: 1},
        compiler_params=params(20),
        cost_estimate=pl.CostEstimate(
            flops=6 * size * size * elems, transcendentals=0, bytes_accessed=4 * 4 * nvar * modes * elems
        ),
        name="main",
    )(
        in_hbm(flux_jacobian_list.transpose(1, 0, 2)), in_hbm(penalty), jacobian_row,
        in_hbm(volume_operator_list), in_hbm(current_state), in_hbm(state_old), in_hbm(second_rim),
    )
    after_main = second_rim
    second_rim = swap(second_rim, "px", 1)

    terms = shaped((peers, nvar, SUBS, LANES), F32)
    groups = cuts // SUBS
    blocks = pltpu.VMEM((groups, modes, SUBS, modes), F32)
    results_out = pl.pallas_call(
        cut_kernel,
        grid=(1,),
        out_shape=terms,
        in_specs=[scalars(), kept(), remote(), remote(), remote()],
        out_specs=whole(terms),
        scratch_shapes=[
            blocks,
            blocks,
            pltpu.VMEM((cuts, 4 * SUBS, LANES), F32),
            pltpu.VMEM((cuts, SUBS, LANES), F32),
            pltpu.SMEM((cuts,), jnp.int32),
            pltpu.SMEM((peers,), jnp.int32),
            pltpu.SemaphoreType.DMA((2, groups)),
        ],
        compiler_params=params(10),
        name="cut",
    )(
        in_hbm(cut_owner.reshape(cuts)), replies,
        in_hbm(cut_mass.transpose(1, 0, 2)), in_hbm(cut_operator.transpose(1, 0, 2)), in_hbm(after_main),
    )
    results = exchange(results_out)

    residual = pl.pallas_call(
        functools.partial(body_kernel, bodies, count, share),
        grid=(1,),
        out_shape=field,
        in_specs=[kept(), whole(stack), whole(square), kept()],
        out_specs=kept(),
        scratch_shapes=[
            pltpu.VMEM((pad8(peers * share), LANES), F32),
            pltpu.VMEM((2, bodies, LANES, LANES), BF16),
            scratch,
            pltpu.VMEM((size, wide), BF16),
        ],
        input_output_aliases={3: 0},
        compiler_params=params(6),
        name="body",
    )(replies, in_hbm(covered_rows), in_hbm(covered_column), in_vmem(residual))

    return pl.pallas_call(
        last_kernel,
        grid=(1,),
        out_shape=shaped(current_state.shape, F32),
        in_specs=[scalars(), kept(), whole(column), kept(), kept(), kept()],
        out_specs=remote(),
        scratch_shapes=[
            pltpu.VMEM(current_state.shape, F32),
            pltpu.VMEM((size, 2 * slots), BF16),
            pltpu.VMEM((2, nvar, LANES, LANES), F32),
            pltpu.SemaphoreType.DMA((nvar * (elems // wide),)),
        ],
        compiler_params=params(8),
        name="last",
    )(in_hbm(penalty), results, in_hbm(slot_column), first_rim, second_rim, in_vmem(residual))


def solution(mesh):
    both = ("px", "py")
    in_specs = (
        P(None, None, both),
        P(None, None, both),
        P(both),
        P(),
        P(),
        P(),
        P(both, None),
        P(both),
        P(both, None, None),
        P(both, None, None),
        P("px"),
        P(both, None, None),
        P(both, None, None),
        P(both, None),
        P(both, None),
    )
    return jax.shard_map(
        local, mesh=mesh, in_specs=in_specs, out_specs=P(None, None, both), check_vma=False
    )
```

```python
import functools

import jax
import jax.numpy as jnp
from jax import lax
from jax.experimental import pallas as pl
from jax.experimental.pallas import tpu as pltpu
from jax.sharding import PartitionSpec as P

DEGREE = 4
LAYERS = 8
LANES = 128
SUBS = 8
MIB = 1 << 20

F32 = jnp.float32
BF16 = jnp.bfloat16
NN = (((1,), (0,)), ((), ()))
NT = (((1,), (1,)), ((), ()))


def pad8(count):
    return -(-count // SUBS) * SUBS


def iota(shape, dim):
    return lax.broadcasted_iota(jnp.int32, shape, dim)


def halves(value):
    high = value.astype(BF16)
    return high, (value - high.astype(F32)).astype(BF16)


def mxu(left, right, dims=NN):
    return lax.dot_general(left, right, dims, preferred_element_type=F32)


def product(left, right, dims=NN):
    left_high, left_low = left
    right_high, right_low = right
    return mxu(left_high, right_high, dims) + (
        mxu(left_low, right_high, dims) + mxu(left_high, right_low, dims)
    )


def exact_dot(left, right, dims=NN):
    return lax.dot_general(
        left, right, dims, precision=lax.Precision.HIGHEST, preferred_element_type=F32
    )


def pick_lanes(values, lanes):
    return jnp.take_along_axis(values, jnp.broadcast_to(lanes, values.shape), axis=1)


def params(limit):
    return pltpu.CompilerParams(vmem_limit_bytes=limit * MIB)


def kept():
    return pl.BlockSpec(memory_space=pltpu.VMEM)


def scalars():
    return pl.BlockSpec(memory_space=pltpu.SMEM)


def remote():
    return pl.BlockSpec(memory_space=pl.ANY)


def in_hbm(array):
    return pltpu.with_memory_space_constraint(array, pltpu.HBM)


def in_vmem(array):
    return pltpu.with_memory_space_constraint(array, pltpu.VMEM)


def stored(array):
    return pltpu.HBM(array.shape, array.dtype)


def whole(array):
    return pl.BlockSpec(array.shape, lambda *_: (0,) * len(array.shape))


def trace_sums(ref, var, first, width):
    face = ref.shape[1] // (DEGREE + 1)
    part = [ref[var, i * face : (i + 1) * face, first : first + width] for i in range(DEGREE + 1)]
    even, odd = (part[0] + part[2]) + part[4], part[1] + part[3]
    return even + odd, even - odd


def ids_kernel(cap, share, hold_ref, owner_ref, elem_ref, points_ref, normals_ref, weights_ref, out_ref, rows_ref):
    peers = out_ref.shape[0]
    bodies = points_ref.shape[0]
    cuts = owner_ref.shape[1]
    me = lax.axis_index("py")
    owner = owner_ref[...]
    named = (owner == iota((pad8(peers), cuts), 0)).astype(F32)
    earlier = (iota((cuts, cuts), 0) < iota((cuts, cuts), 1)).astype(F32)
    place = jnp.sum(mxu(named, earlier) * named, axis=0, keepdims=True).astype(jnp.int32)
    compact = (owner * cap + place == iota((LANES, cuts), 0)).astype(F32)
    ids = exact_dot(elem_ref[...].astype(F32) + 1.0, compact, NT) - 1.0
    rows_ref[...] = jnp.zeros_like(rows_ref)
    for body in range(bodies):
        mine = hold_ref[body] == me
        rows_ref[body * 7 : body * 7 + 3] = jnp.where(mine, points_ref[body], 0.0)
        rows_ref[body * 7 + 3 : body * 7 + 6] = jnp.where(mine, normals_ref[body], 0.0)
        rows_ref[body * 7 + 6 : body * 7 + 7] = jnp.where(mine, weights_ref[body : body + 1], 0.0)
    for peer in range(peers):
        out_ref[peer] = jnp.zeros((SUBS, LANES), F32)
        out_ref[peer, 0:1] = ids
        out_ref[peer, 1 : 1 + share] = rows_ref[peer * share : (peer + 1) * share]


def load_kernel(
    covered_hbm, state_hbm, state_ref, first_ref, second_ref, rows_ref, column_ref, covered_ref, acc_ref, sems
):
    even = lax.axis_index("px") % 2 == 0
    nvar, modes, elems = state_ref.shape
    face = modes // (DEGREE + 1)
    bodies, count = covered_ref.shape
    copies = [pltpu.make_async_copy(state_hbm.at[var], state_ref.at[var], sems.at[var]) for var in range(nvar)]
    covered_copy = pltpu.make_async_copy(covered_hbm, covered_ref, sems.at[nvar])
    covered_copy.start()
    for copy in copies:
        copy.start()
    acc_ref[...] = jnp.zeros_like(acc_ref)
    first_ref[...] = jnp.zeros_like(first_ref)
    second_ref[...] = jnp.zeros_like(second_ref)
    covered_copy.wait()

    spread = (iota((count, LANES), 1) % count == iota((count, LANES), 0)).astype(F32)
    tiled = exact_dot(covered_ref[...].astype(F32), spread)
    mine = iota((bodies, LANES), 1) // count == iota((bodies, LANES), 0)
    row = jnp.sum(jnp.where(mine, tiled + 1.0, 0.0), axis=0, keepdims=True) - 1.0
    column_ref[...] = jnp.broadcast_to(row, (LANES, LANES)).T.astype(jnp.int32)
    spots = row.astype(jnp.int32)
    for var in range(nvar):
        copies[var].wait()
        lower = trace_sums(state_ref, var, 0, LANES)[1]
        upper = trace_sums(state_ref, var, elems - LANES, LANES)[0]
        first_ref[var, :face] = jnp.where(even, upper, lower)
        second_ref[var, :face] = jnp.where(even, lower, upper)
        found = acc_ref[var, :modes]
        for layer in range(elems // LANES):
            lanes = slice(layer * LANES, (layer + 1) * LANES)
            picked = pick_lanes(state_ref[var, :, lanes], spots & (LANES - 1))
            found = jnp.where((spots + LANES) // LANES == layer + 1, picked, found)
        acc_ref[var, :modes] = found
        rows_ref[var] = acc_ref[var].T


def pick_kernel(cap, share, got_ref, state_ref, old_hbm, out_ref, column_ref, old_ref, acc_ref, sems):
    nvar, modes, elems = state_ref.shape
    peers = got_ref.shape[0]
    half = LANES // 2
    copies = [pltpu.make_async_copy(old_hbm.at[var], old_ref.at[var], sems.at[var]) for var in range(nvar)]
    for copy in copies:
        copy.start()
    lane = iota((1, LANES), 1)
    me = lax.axis_index("py")
    row = jnp.zeros((1, LANES), F32) - 1.0
    for peer in range(peers):
        moved = pltpu.roll(got_ref[peer, 0:1], ((peer - me) * cap + LANES) % LANES, 1)
        row = jnp.where(lane // cap == peer, moved, row)
    row = jnp.where(lane < half, row, pltpu.roll(row, half, 1))
    spots = row.astype(jnp.int32)
    acc_ref[...] = jnp.zeros_like(acc_ref)

    def gather(ref, var, wanted):
        found = acc_ref[var, :modes]
        for layer in range(elems // LANES):
            picked = pick_lanes(ref[var, :, layer * LANES : (layer + 1) * LANES], spots & (LANES - 1))
            found = jnp.where(wanted & ((spots + LANES) // LANES == layer + 1), picked, found)
        acc_ref[var, :modes] = found

    for var in range(nvar):
        gather(state_ref, var, lane < half)
    data = got_ref[0]
    for peer in range(1, peers):
        data = data + got_ref[peer]
    for peer in range(peers):
        out_ref[peer, 2 * nvar, :, :] = data
    column = jnp.broadcast_to(row, (LANES, LANES)).T.astype(jnp.int32)
    if cap < SUBS:
        column_ref[...] = jnp.zeros_like(column_ref) - 1
    for peer in range(peers):
        column_ref[peer * SUBS : peer * SUBS + cap] = column[peer * cap : (peer + 1) * cap]
    for var in range(nvar):
        copies[var].wait()
        gather(old_ref, var, lane >= half)
        rows = acc_ref[var].T
        for peer in range(peers):
            for kind in range(2):
                first = kind * half + peer * cap
                if cap < SUBS:
                    out_ref[peer, kind * nvar + var] = jnp.zeros((SUBS, LANES), F32)
                out_ref[peer, kind * nvar + var, :cap] = rows[first : first + cap]


def main_kernel(
    flux_hbm, penalty_hbm, jac_hbm, operator_hbm, state_hbm, old_hbm, _,
    out_ref, _unused, flux_ref, penalty_ref, jac_ref, state_ref, old_ref, operator_ref, padded_ref, matrix_ref, right_ref, product_ref, face_ref, sems,
):
    nvar, modes, elems = state_ref.shape
    degree_one = DEGREE + 1
    face = modes // degree_one
    size = nvar * LANES
    width = face_ref.shape[2]
    copies = [
        pltpu.make_async_copy(source, target, sems.at[index])
        for index, (source, target) in enumerate(
            (
                (operator_hbm, operator_ref),
                (state_hbm, state_ref),
                (old_hbm, old_ref),
                (flux_hbm, flux_ref),
                (penalty_hbm, penalty_ref),
                (jac_hbm, jac_ref),
            )
        )
    ]
    for index in (3, 4, 0, 1, 5):
        copies[index].start()
    padded_ref[...] = jnp.zeros_like(padded_ref)
    gap = LANES - modes
    for var in range(nvar):
        for place in (0, size):
            last = place + var * LANES + modes
            right_ref[:, last : last + gap] = jnp.zeros((right_ref.shape[0], gap, width), BF16)

    def digits(index):
        high = jnp.floor((index + 0.5) * (1.0 / face))
        return high, index - face * high

    row_high, row_low = digits(iota((LANES, LANES), 0).astype(F32))
    col_high, col_low = digits(iota((LANES, LANES), 1).astype(F32))
    apart = row_high - col_high
    apart = apart - 2.0 * jnp.floor(0.5 * apart)
    inside = iota((LANES, LANES), 0) < modes
    own_face = jnp.where((row_low == col_low) & (apart == 0.0) & inside, 2.0, 0.0)
    own_face = jnp.where(iota((LANES, LANES), 1) < modes, own_face, 0.0)
    for index in (3, 4, 0):
        copies[index].wait()
    copies[2].start()
    padded_ref[:, :modes, :modes] = operator_ref[...]
    for var in range(nvar):
        for other in range(nvar):
            block = -(flux_ref[var, 0, other] * padded_ref[0])
            for direction in range(1, 3):
                block = block - flux_ref[var, direction, other] * padded_ref[direction]
            if var == other:
                block = block + penalty_ref[var] * own_face
            high, low = halves(block)
            rows = slice(var * LANES, (var + 1) * LANES)
            for place, part in ((0, high), (size, high), (2 * size, low)):
                matrix_ref[rows, place + other * LANES : place + (other + 1) * LANES] = part
    mid = jnp.floor((row_low + 0.5) * (1.0 / degree_one))
    weight = 8.0 / (
        (2.0 * row_high + 1.0) * (2.0 * mid + 1.0) * (2.0 * (row_low - degree_one * mid) + 1.0)
    )
    weight = jnp.concatenate([weight] * (width // LANES), axis=1)[:modes]

    def split(chunk):
        for var in range(nvar):
            high, low = halves(state_ref[var, :, chunk * width : (chunk + 1) * width])
            for place, part in ((0, high), (size, low)):
                right_ref[chunk % 2, place + var * LANES : place + var * LANES + modes] = part

    def multiply(chunk):
        product_ref[chunk % 2] = mxu(matrix_ref[:, : 2 * size], right_ref[chunk % 2]) + mxu(
            matrix_ref[:, 2 * size :], right_ref[chunk % 2, :size]
        )

    copies[1].wait()
    split(0)
    multiply(0)
    split(1)
    copies[5].wait()
    copies[2].wait()
    below = [jnp.zeros((face, LANES), F32)] * nvar
    chunks = elems // width
    for chunk in range(chunks):
        first = chunk * width
        lanes = slice(first, first + width)
        if chunk + 1 < chunks:
            multiply(chunk + 1)
        if chunk + 2 < chunks:
            split(chunk + 2)
        scale = weight * jac_ref[:, lanes]
        for var in range(nvar):
            upper, lower = trace_sums(state_ref, var, first, width)
            if chunk + 1 < chunks:
                above = trace_sums(state_ref, var, first + width, LANES)[1]
            else:
                above = jnp.zeros((face, LANES), F32)
            above = jnp.concatenate([lower[:, LANES:], above], axis=1)
            under = jnp.concatenate([below[var], upper[:, : width - LANES]], axis=1)
            below[var] = upper[:, width - LANES :]
            plus = penalty_ref[var] * (above + under)
            minus = penalty_ref[var] * (above - under)
            for i in range(degree_one):
                face_ref[var, i * face : (i + 1) * face] = minus if i % 2 else plus
            change = state_ref[var, :, lanes] - old_ref[var, :, lanes]
            out_ref[var, :, lanes] = (
                product_ref[chunk % 2, var * LANES : var * LANES + modes] + scale * change
            ) - face_ref[var, :modes]


def cut_kernel(
    owner_hbm, got_ref, mass_hbm, operator_hbm, _, out_ref, owner_ref, mass_ref, operator_ref, left_ref, term_ref,
    spot_ref, seen_ref, sems,
):
    groups, modes = mass_ref.shape[:2]
    peers, nvar = out_ref.shape[0], out_ref.shape[1]
    kinds = got_ref.shape[1]
    owner_copy = pltpu.make_async_copy(owner_hbm, owner_ref, sems.at[0, groups])
    owner_copy.start()
    copies = []
    for group in range(groups):
        rows = slice(group * SUBS, (group + 1) * SUBS)
        copies.append(
            (
                pltpu.make_async_copy(mass_hbm.at[:, rows], mass_ref.at[group], sems.at[0, group]),
                pltpu.make_async_copy(operator_hbm.at[:, rows], operator_ref.at[group], sems.at[1, group]),
            )
        )
        for copy in copies[-1]:
            copy.start()
    out_ref[...] = jnp.zeros_like(out_ref)
    for peer in range(peers):
        seen_ref[peer] = 0
    owner_copy.wait()
    got = got_ref.reshape(peers * kinds * SUBS, LANES)
    out = out_ref.reshape(peers * nvar * SUBS, LANES)
    for index in range(groups * SUBS):
        owner = owner_ref[index]
        place = seen_ref[owner]
        seen_ref[owner] = place + 1
        spot_ref[index] = owner * (nvar * SUBS) + place
        first = owner * (kinds * SUBS) + place
        states = got[pl.ds(first, nvar, stride=SUBS), :]
        changes = states - got[pl.ds(first + nvar * SUBS, nvar, stride=SUBS), :]
        for kind, value in enumerate((changes, -states)):
            lanes = slice(kind * LANES, (kind + 1) * LANES)
            high = value.astype(BF16).astype(F32)
            left_ref[index, :nvar, lanes] = high
            left_ref[index, SUBS : SUBS + nvar, lanes] = value - high
    zero = jnp.zeros((modes, LANES - modes), F32)
    for group in range(groups):
        for copy in copies[group]:
            copy.wait()
        for inner in range(SUBS):
            index = group * SUBS + inner
            blocks = []
            for ref in (mass_ref, operator_ref):
                block = ref.at[group].reshape(modes * SUBS, modes)[pl.ds(inner, modes, stride=SUBS), :]
                blocks.append(jnp.concatenate([block, zero], axis=1))
            high, low = halves(jnp.concatenate(blocks, axis=1))
            left = left_ref[index].astype(BF16)
            total = mxu(left, high, NT) + mxu(left, low, NT)
            term_ref[index, :, :modes] = total[:SUBS] + total[SUBS:]
    for index in range(groups * SUBS):
        out[pl.ds(spot_ref[index], nvar, stride=SUBS), :modes] = term_ref[index, :nvar, :modes]


def body_kernel(bodies, count, share, got_ref, rows_ref, column_ref, base_ref, out_ref, data_ref, basis_ref, lift_ref, left_ref):
    peers = got_ref.shape[0]
    nvar, modes, elems = out_ref.shape
    degree_one = DEGREE + 1
    for peer in range(peers):
        data_ref[peer * share : (peer + 1) * share] = got_ref[peer, 2 * nvar, 1 : 1 + share]
    lift_ref[...] = jnp.zeros_like(lift_ref)
    mode, degree = iota((LANES, SUBS), 0), iota((LANES, SUBS), 1)
    real = mode < modes
    spreads = []
    for digit in (mode // (degree_one * degree_one), mode // degree_one % degree_one, mode % degree_one):
        chosen = (real & (digit == degree)).astype(BF16)
        spreads.append(jnp.concatenate([chosen, chosen, chosen], axis=1))
    ones = jnp.ones((1, LANES), F32)
    none = jnp.zeros((SUBS - degree_one, LANES), F32)
    for body in range(bodies):
        basis = None
        for axis in range(3):
            coords = data_ref[body * 7 + axis : body * 7 + axis + 1]
            table = [ones, coords]
            for n in range(1, DEGREE):
                table.append(((2.0 * n + 1.0) * coords * table[n] - n * table[n - 1]) / (n + 1.0))
            stacked = jnp.concatenate(table + [none], axis=0)
            high = stacked.astype(BF16)
            middle, low = halves(stacked - high.astype(F32))
            factor = mxu(spreads[axis], jnp.concatenate([high, middle, low], axis=0))
            basis = factor if basis is None else basis * factor
        basis_ref[0, body], basis_ref[1, body] = halves(basis)
    bases = [(basis_ref[0, body], basis_ref[1, body]) for body in range(bodies)]
    traces = []
    for body in range(bodies):
        rows = jnp.concatenate([rows_ref[var, body * count : (body + 1) * count] for var in range(nvar)], axis=0)
        traces.append(product(halves(rows), bases[body]))
    fluxes = []
    for body in range(bodies):
        trace = [traces[body][var * count : (var + 1) * count] for var in range(nvar)]
        normal = [data_ref[body * 7 + 3 + axis : body * 7 + 4 + axis] for axis in range(3)]
        weights = data_ref[body * 7 + 6 : body * 7 + 7]
        speed = normal[0] * trace[1] + normal[1] * trace[2] + normal[2] * trace[3]
        flux = [speed + 0.5 * trace[0]] + [normal[axis] * trace[4] for axis in range(3)] + [1.4 * speed]
        fluxes.append(halves(jnp.concatenate([part * weights for part in flux], axis=0)))
    for body in range(bodies):
        lifted = product(fluxes[body], bases[body], NT)
        for var in range(nvar):
            lift_ref[var, body * count : (body + 1) * count] = lifted[var * count : (var + 1) * count]
    for var in range(nvar):
        high, low = halves(lift_ref[var].T)
        left_ref[var * LANES : (var + 1) * LANES, :LANES] = high
        left_ref[var * LANES : (var + 1) * LANES, LANES:] = low

    width = 2 * LANES
    spots = jnp.concatenate([column_ref[...]] * (width // LANES), axis=1)
    for first in range(0, elems, width):
        chosen = (spots == iota((LANES, width), 1) + first).astype(BF16)
        added = mxu(left_ref[...], jnp.concatenate([chosen, chosen], axis=0))
        for var in range(nvar):
            lanes = slice(first, first + width)
            out_ref[var, :, lanes] = base_ref[var, :, lanes] - added[var * LANES : var * LANES + modes]


def rim_kernel(penalty_ref, first_ref, second_ref, base_ref, out_ref, face_ref):
    nvar, modes, elems = out_ref.shape
    degree_one = DEGREE + 1
    face = modes // degree_one
    even = lax.axis_index("px") % 2 == 0
    bottom, top = slice(0, LANES), slice(elems - LANES, elems)
    for var in range(nvar):
        first, second = first_ref[var, :face], second_ref[var, :face]
        above = penalty_ref[var] * jnp.where(even, first, second)
        below = penalty_ref[var] * jnp.where(even, second, first)
        for i in range(degree_one):
            face_ref[0, var, i * face : (i + 1) * face] = -below if i % 2 else below
            face_ref[1, var, i * face : (i + 1) * face] = above
    for var in range(nvar):
        out_ref[var, :, bottom] = base_ref[var, :, bottom] - face_ref[0, var, :modes]
        out_ref[var, :, top] = base_ref[var, :, top] - face_ref[1, var, :modes]


def last_kernel(got_ref, column_ref, base_ref, out_hbm, out_ref, left_ref, sems):
    nvar, modes, elems = out_ref.shape
    slots = column_ref.shape[0]
    width = 2 * LANES
    for var in range(nvar):
        rows = got_ref[:, var].reshape(slots, LANES).T
        left_ref[var * LANES : (var + 1) * LANES] = jnp.concatenate(halves(rows), axis=1)
    spots = jnp.concatenate([column_ref[...]] * (width // LANES), axis=1)
    copies = []
    for start in range(0, elems, width):
        lanes = slice(start, start + width)
        chosen = (spots == iota((slots, width), 1) + start).astype(BF16)
        added = mxu(left_ref[...], jnp.concatenate([chosen, chosen], axis=0))
        for var in range(nvar):
            out_ref[var, :, lanes] = base_ref[var, :, lanes] + added[var * LANES : var * LANES + modes]
            copies.append(
                pltpu.make_async_copy(out_ref.at[var, :, lanes], out_hbm.at[var, :, lanes], sems.at[len(copies)])
            )
            copies[-1].start()
    for copy in copies:
        copy.wait()


def swap(value, axis, odd):
    count = lax.axis_size(axis)
    pairs = [(low, low + 1) for low in range(odd, count - 1, 2)]
    return lax.ppermute(value, axis, pairs + [(high, low) for low, high in pairs])


def exchange(value):
    return lax.all_to_all(value, "py", split_axis=0, concat_axis=0, tiled=True)


def local(
    current_state, state_old, jacobian, volume_operator_list, flux_jacobian_list, penalty, cut_owner, cut_element,
    cut_mass, cut_operator, body_holder_index, body_points, body_normals, body_weights, covered,
):
    nvar, modes, elems = current_state.shape
    columns = elems // LAYERS
    face = modes // (DEGREE + 1)
    peers = lax.axis_size("py")
    cuts = cut_owner.shape[0]
    bodies, count = covered.shape
    cap = max(2, cuts * 3 // (2 * peers) + 1)
    share = -(-bodies * 7 // peers)
    half = LANES // 2
    slots = peers * SUBS
    assert columns == LANES and peers * cap <= half and bodies * count <= LANES
    assert cap <= SUBS and 1 + share <= SUBS and modes <= LANES and cuts % SUBS == 0
    shaped = jax.ShapeDtypeStruct
    wide = 2 * LANES
    size = nvar * LANES

    owner_row = in_hbm(cut_owner.reshape(1, cuts))
    small = [in_hbm(array) for array in (cut_element.reshape(1, cuts), body_points, body_normals, body_weights)]
    asked = shaped((peers, SUBS, LANES), F32)
    asked = pl.pallas_call(
        functools.partial(ids_kernel, cap, share),
        grid=(1,),
        out_shape=pltpu.VMEM(asked.shape, F32),
        in_specs=[scalars(), whole(owner_row)] + [whole(array) for array in small],
        out_specs=kept(),
        scratch_shapes=[pltpu.VMEM((pad8(peers * share), LANES), F32)],
        compiler_params=params(4),
        name="ids",
    )(in_hbm(body_holder_index), owner_row, *small)
    requests = exchange(asked)

    field = pltpu.VMEM(current_state.shape, F32)
    face_rows = shaped((nvar, pad8(face), LANES), F32)
    stack = shaped((nvar, LANES, LANES), F32)
    square = shaped((LANES, LANES), jnp.int32)
    scratch = pltpu.VMEM(stack.shape, F32)
    state, first_rim, second_rim, covered_rows, covered_column = pl.pallas_call(
        load_kernel,
        grid=(1,),
        out_shape=(field, face_rows, stored(face_rows), stored(stack), stored(square)),
        in_specs=[remote(), remote()],
        out_specs=(kept(), whole(face_rows), whole(face_rows), whole(stack), whole(square)),
        scratch_shapes=[
            pltpu.VMEM(covered.shape, jnp.int32),
            scratch,
            pltpu.SemaphoreType.DMA((nvar + 1,)),
        ],
        compiler_params=params(4),
        name="load",
    )(in_hbm(covered), in_hbm(current_state))
    first_rim = swap(first_rim, "px", 0)

    reply = shaped((peers, 2 * nvar + 1, SUBS, LANES), F32)
    column = shaped((slots, LANES), jnp.int32)
    states_out, slot_column = pl.pallas_call(
        functools.partial(pick_kernel, cap, share),
        grid=(1,),
        out_shape=(pltpu.VMEM(reply.shape, F32), pltpu.VMEM(column.shape, column.dtype)),
        in_specs=[kept(), kept(), remote()],
        out_specs=(kept(), kept()),
        scratch_shapes=[pltpu.VMEM(current_state.shape, F32), scratch, pltpu.SemaphoreType.DMA((nvar,))],
        compiler_params=params(6),
        name="pick",
    )(requests, in_vmem(state), in_hbm(state_old))
    replies = exchange(states_out)

    jacobian_row = in_hbm(jacobian.reshape(1, elems))
    residual, second_rim = pl.pallas_call(
        main_kernel,
        grid=(1,),
        out_shape=(field, stored(face_rows)),
        in_specs=[remote()] * 7,
        out_specs=(kept(), remote()),
        scratch_shapes=[
            pltpu.SMEM((nvar, 3, nvar), F32),
            pltpu.SMEM((nvar,), F32),
            pltpu.VMEM((1, elems), F32),
            pltpu.VMEM(current_state.shape, F32),
            pltpu.VMEM(current_state.shape, F32),
            pltpu.VMEM(volume_operator_list.shape, F32),
            pltpu.VMEM((3, LANES, LANES), F32),
            pltpu.VMEM((size, 3 * size), BF16),
            pltpu.VMEM((2, 2 * size, wide), BF16),
            pltpu.VMEM((2, size, wide), F32),
            pltpu.VMEM((nvar, LANES, wide), F32),
            pltpu.SemaphoreType.DMA((6,)),
        ],
        input_output_aliases={6: 1},
        compiler_params=params(20),
        cost_estimate=pl.CostEstimate(
            flops=6 * size * size * elems, transcendentals=0, bytes_accessed=4 * 4 * nvar * modes * elems
        ),
        name="main",
    )(
        in_hbm(flux_jacobian_list.transpose(1, 0, 2)), in_hbm(penalty), jacobian_row,
        in_hbm(volume_operator_list), in_hbm(current_state), in_hbm(state_old), in_hbm(second_rim),
    )
    after_main = second_rim
    second_rim = swap(second_rim, "px", 1)

    terms = shaped((peers, nvar, SUBS, LANES), F32)
    groups = cuts // SUBS
    blocks = pltpu.VMEM((groups, modes, SUBS, modes), F32)
    results_out = pl.pallas_call(
        cut_kernel,
        grid=(1,),
        out_shape=pltpu.VMEM(terms.shape, F32),
        in_specs=[remote(), kept(), remote(), remote(), remote()],
        out_specs=kept(),
        scratch_shapes=[
            pltpu.SMEM((cuts,), jnp.int32),
            blocks,
            blocks,
            pltpu.VMEM((cuts, 2 * SUBS, 2 * LANES), F32),
            pltpu.VMEM((cuts, SUBS, LANES), F32),
            pltpu.SMEM((cuts,), jnp.int32),
            pltpu.SMEM((peers,), jnp.int32),
            pltpu.SemaphoreType.DMA((2, groups + 1)),
        ],
        compiler_params=params(10),
        name="cut",
    )(
        in_hbm(cut_owner.reshape(cuts)), replies,
        in_hbm(cut_mass.transpose(1, 0, 2)), in_hbm(cut_operator.transpose(1, 0, 2)), in_hbm(after_main),
    )
    results = exchange(results_out)

    residual = pl.pallas_call(
        functools.partial(body_kernel, bodies, count, share),
        grid=(1,),
        out_shape=field,
        in_specs=[kept(), whole(stack), whole(square), kept()],
        out_specs=kept(),
        scratch_shapes=[
            pltpu.VMEM((pad8(peers * share), LANES), F32),
            pltpu.VMEM((2, bodies, LANES, LANES), BF16),
            scratch,
            pltpu.VMEM((size, wide), BF16),
        ],
        input_output_aliases={3: 0},
        compiler_params=params(6),
        name="body",
    )(replies, in_hbm(covered_rows), in_hbm(covered_column), in_vmem(residual))

    residual = pl.pallas_call(
        rim_kernel,
        grid=(1,),
        out_shape=field,
        in_specs=[scalars()] + [kept()] * 3,
        out_specs=kept(),
        scratch_shapes=[pltpu.VMEM((2, nvar, LANES, LANES), F32)],
        input_output_aliases={3: 0},
        compiler_params=params(2),
        name="rim",
    )(in_hbm(penalty), first_rim, second_rim, in_vmem(residual))

    return pl.pallas_call(
        last_kernel,
        grid=(1,),
        out_shape=shaped(current_state.shape, F32),
        in_specs=[kept(), kept(), kept()],
        out_specs=remote(),
        scratch_shapes=[
            pltpu.VMEM(current_state.shape, F32),
            pltpu.VMEM((size, 2 * slots), BF16),
            pltpu.SemaphoreType.DMA((nvar * (elems // wide),)),
        ],
        compiler_params=params(8),
        name="last",
    )(results, in_vmem(slot_column), in_vmem(residual))


def solution(mesh):
    both = ("px", "py")
    in_specs = (
        P(None, None, both),
        P(None, None, both),
        P(both),
        P(),
        P(),
        P(),
        P(both, None),
        P(both),
        P(both, None, None),
        P(both, None, None),
        P("px"),
        P(both, None, None),
        P(both, None, None),
        P(both, None),
        P(both, None),
    )
    return jax.shard_map(
        local, mesh=mesh, in_specs=in_specs, out_specs=P(None, None, both), check_vma=False
    )
```

```python
import functools

import jax
import jax.numpy as jnp
from jax import lax
from jax.experimental import pallas as pl
from jax.experimental.pallas import tpu as pltpu
from jax.sharding import PartitionSpec as P


DEGREE = 4
LAYERS = 8
LANES = 128
SUBS = 8
MIB = 1 << 20

F32 = jnp.float32
BF16 = jnp.bfloat16
NN = (((1,), (0,)), ((), ()))
NT = (((1,), (1,)), ((), ()))


def pad8(count):
    return -(-count // SUBS) * SUBS


def iota(shape, dim):
    return lax.broadcasted_iota(jnp.int32, shape, dim)


def halves(value):
    high = value.astype(BF16)
    return high, (value - high.astype(F32)).astype(BF16)


def mxu(left, right, dims=NN):
    return lax.dot_general(left, right, dims, preferred_element_type=F32)


def product(left, right, dims=NN):
    left_high, left_low = left
    right_high, right_low = right
    return mxu(left_high, right_high, dims) + (
        mxu(left_low, right_high, dims) + mxu(left_high, right_low, dims)
    )


def exact_dot(left, right, dims=NN):
    return lax.dot_general(
        left, right, dims, precision=lax.Precision.HIGHEST, preferred_element_type=F32
    )


def pick_lanes(values, lanes):
    return jnp.take_along_axis(values, jnp.broadcast_to(lanes, values.shape), axis=1)


def params(limit):
    return pltpu.CompilerParams(vmem_limit_bytes=limit * MIB)


def kept():
    return pl.BlockSpec(memory_space=pltpu.VMEM)


def scalars():
    return pl.BlockSpec(memory_space=pltpu.SMEM)


def remote():
    return pl.BlockSpec(memory_space=pl.ANY)


def in_hbm(array):
    return pltpu.with_memory_space_constraint(array, pltpu.HBM)


def in_vmem(array):
    return pltpu.with_memory_space_constraint(array, pltpu.VMEM)


def stored(array):
    return pltpu.HBM(array.shape, array.dtype)


def whole(array):
    return pl.BlockSpec(array.shape, lambda *_: (0,) * len(array.shape))


def trace_sums(ref, var, first, width):
    face = ref.shape[1] // (DEGREE + 1)
    part = [ref[var, i * face : (i + 1) * face, first : first + width] for i in range(DEGREE + 1)]
    even, odd = (part[0] + part[2]) + part[4], part[1] + part[3]
    return even + odd, even - odd


def ids_kernel(cap, share, hold_ref, owner_ref, elem_ref, points_ref, normals_ref, weights_ref, out_ref, rows_ref):
    peers = out_ref.shape[0]
    bodies = points_ref.shape[0]
    cuts = owner_ref.shape[1]
    me = lax.axis_index("py")
    owner = owner_ref[...]
    named = (owner == iota((pad8(peers), cuts), 0)).astype(F32)
    earlier = (iota((cuts, cuts), 0) < iota((cuts, cuts), 1)).astype(F32)
    place = jnp.sum(mxu(named, earlier) * named, axis=0, keepdims=True).astype(jnp.int32)
    compact = (owner * cap + place == iota((LANES, cuts), 0)).astype(F32)
    ids = exact_dot(elem_ref[...].astype(F32) + 1.0, compact, NT) - 1.0
    rows_ref[...] = jnp.zeros_like(rows_ref)
    for body in range(bodies):
        mine = hold_ref[body] == me
        rows_ref[body * 7 : body * 7 + 3] = jnp.where(mine, points_ref[body], 0.0)
        rows_ref[body * 7 + 3 : body * 7 + 6] = jnp.where(mine, normals_ref[body], 0.0)
        rows_ref[body * 7 + 6 : body * 7 + 7] = jnp.where(mine, weights_ref[body : body + 1], 0.0)
    for peer in range(peers):
        out_ref[peer] = jnp.zeros((SUBS, LANES), F32)
        out_ref[peer, 0:1] = ids
        out_ref[peer, 1 : 1 + share] = rows_ref[peer * share : (peer + 1) * share]


def load_kernel(
    covered_hbm, state_hbm, operator_hbm, flux_hbm, penalty_hbm,
    state_ref, first_ref, second_ref, rows_ref, column_ref, operator_ref, flux_ref, penalty_ref,
    covered_ref, acc_ref, sems,
):
    even = lax.axis_index("px") % 2 == 0
    nvar, modes, elems = state_ref.shape
    face = modes // (DEGREE + 1)
    bodies, count = covered_ref.shape
    copies = [pltpu.make_async_copy(state_hbm.at[var], state_ref.at[var], sems.at[var]) for var in range(nvar)]
    covered_copy = pltpu.make_async_copy(covered_hbm, covered_ref, sems.at[nvar])
    covered_copy.start()
    for copy in copies:
        copy.start()
    small = [
        pltpu.make_async_copy(source, target, sems.at[nvar + 1 + index])
        for index, (source, target) in enumerate(
            ((operator_hbm, operator_ref), (flux_hbm, flux_ref), (penalty_hbm, penalty_ref))
        )
    ]
    for copy in small:
        copy.start()
    acc_ref[...] = jnp.zeros_like(acc_ref)
    first_ref[...] = jnp.zeros_like(first_ref)
    second_ref[...] = jnp.zeros_like(second_ref)
    covered_copy.wait()

    spread = (iota((count, LANES), 1) % count == iota((count, LANES), 0)).astype(F32)
    tiled = exact_dot(covered_ref[...].astype(F32), spread)
    mine = iota((bodies, LANES), 1) // count == iota((bodies, LANES), 0)
    row = jnp.sum(jnp.where(mine, tiled + 1.0, 0.0), axis=0, keepdims=True) - 1.0
    column_ref[...] = jnp.broadcast_to(row, (LANES, LANES)).T.astype(jnp.int32)
    spots = row.astype(jnp.int32)
    for var in range(nvar):
        copies[var].wait()
        lower = trace_sums(state_ref, var, 0, LANES)[1]
        upper = trace_sums(state_ref, var, elems - LANES, LANES)[0]
        first_ref[var, :face] = jnp.where(even, upper, lower)
        second_ref[var, :face] = jnp.where(even, lower, upper)
        found = acc_ref[var, :modes]
        for layer in range(elems // LANES):
            lanes = slice(layer * LANES, (layer + 1) * LANES)
            picked = pick_lanes(state_ref[var, :, lanes], spots & (LANES - 1))
            found = jnp.where((spots + LANES) // LANES == layer + 1, picked, found)
        acc_ref[var, :modes] = found
        rows_ref[var] = acc_ref[var].T
    for copy in small:
        copy.wait()


def pick_kernel(cap, got_ref, state_ref, old_hbm, out_hbm, column_ref, out_ref, old_ref, acc_ref, sems):
    nvar, modes, elems = state_ref.shape
    peers = got_ref.shape[0]
    half = LANES // 2
    copies = [pltpu.make_async_copy(old_hbm.at[var], old_ref.at[var], sems.at[var]) for var in range(nvar)]
    for copy in copies:
        copy.start()
    lane = iota((1, LANES), 1)
    me = lax.axis_index("py")
    row = jnp.zeros((1, LANES), F32) - 1.0
    for peer in range(peers):
        moved = pltpu.roll(got_ref[peer, 0:1], ((peer - me) * cap + LANES) % LANES, 1)
        row = jnp.where(lane // cap == peer, moved, row)
    row = jnp.where(lane < half, row, pltpu.roll(row, half, 1))
    spots = row.astype(jnp.int32)
    acc_ref[...] = jnp.zeros_like(acc_ref)

    def gather(ref, var, wanted):
        found = acc_ref[var, :modes]
        for layer in range(elems // LANES):
            picked = pick_lanes(ref[var, :, layer * LANES : (layer + 1) * LANES], spots & (LANES - 1))
            found = jnp.where(wanted & ((spots + LANES) // LANES == layer + 1), picked, found)
        acc_ref[var, :modes] = found

    for var in range(nvar):
        gather(state_ref, var, lane < half)
    data = got_ref[0]
    for peer in range(1, peers):
        data = data + got_ref[peer]
    sent = []

    def send(kind):
        sent.append(pltpu.make_async_copy(out_ref.at[:, kind], out_hbm.at[:, kind], sems.at[nvar + kind]))
        sent[-1].start()

    for peer in range(peers):
        out_ref[peer, 2 * nvar, :, :] = data
    send(2 * nvar)
    column = jnp.broadcast_to(row, (LANES, LANES)).T.astype(jnp.int32)
    if cap < SUBS:
        column_ref[...] = jnp.zeros_like(column_ref) - 1
    for peer in range(peers):
        column_ref[peer * SUBS : peer * SUBS + cap] = column[peer * cap : (peer + 1) * cap]
    for var in range(nvar):
        copies[var].wait()
        gather(old_ref, var, lane >= half)
        rows = acc_ref[var].T
        for peer in range(peers):
            for kind in range(2):
                first = kind * half + peer * cap
                if cap < SUBS:
                    out_ref[peer, kind * nvar + var] = jnp.zeros((SUBS, LANES), F32)
                out_ref[peer, kind * nvar + var, :cap] = rows[first : first + cap]
        send(var)
        send(nvar + var)
    for copy in sent:
        copy.wait()


def main_kernel(
    flux_vmem, penalty_vmem, operator_ref, _, jac_hbm, old_hbm, owner_hbm, _rim,
    out_ref, owner_ref, _same, flux_ref, penalty_ref, jac_ref, old_ref, padded_ref, matrix_ref, right_ref,
    product_ref, face_ref, sems,
):
    state_ref = out_ref
    nvar, modes, elems = state_ref.shape
    degree_one = DEGREE + 1
    face = modes // degree_one
    size = nvar * LANES
    width = face_ref.shape[2]
    copies = [
        pltpu.make_async_copy(source, target, sems.at[index])
        for index, (source, target) in enumerate(
            (
                (flux_vmem, flux_ref),
                (penalty_vmem, penalty_ref),
                (old_hbm, old_ref),
                (jac_hbm, jac_ref),
                (owner_hbm, owner_ref),
            )
        )
    ]
    for copy in copies:
        copy.start()
    chunks = elems // width
    padded_ref[...] = jnp.zeros_like(padded_ref)
    gap = LANES - modes
    for var in range(nvar):
        for place in (0, size):
            last = place + var * LANES + modes
            right_ref[:, last : last + gap] = jnp.zeros((right_ref.shape[0], gap, width), BF16)

    def digits(index):
        high = jnp.floor((index + 0.5) * (1.0 / face))
        return high, index - face * high

    row_high, row_low = digits(iota((LANES, LANES), 0).astype(F32))
    col_high, col_low = digits(iota((LANES, LANES), 1).astype(F32))
    apart = row_high - col_high
    apart = apart - 2.0 * jnp.floor(0.5 * apart)
    inside = iota((LANES, LANES), 0) < modes
    own_face = jnp.where((row_low == col_low) & (apart == 0.0) & inside, 2.0, 0.0)
    own_face = jnp.where(iota((LANES, LANES), 1) < modes, own_face, 0.0)
    copies[0].wait()
    copies[1].wait()
    padded_ref[:, :modes, :modes] = operator_ref[...]
    for var in range(nvar):
        for other in range(nvar):
            block = -(flux_ref[var, 0, other] * padded_ref[0])
            for direction in range(1, 3):
                block = block - flux_ref[var, direction, other] * padded_ref[direction]
            if var == other:
                block = block + penalty_ref[var] * own_face
            high, low = halves(block)
            rows = slice(var * LANES, (var + 1) * LANES)
            for place, part in ((0, high), (size, high), (2 * size, low)):
                matrix_ref[rows, place + other * LANES : place + (other + 1) * LANES] = part
    mid = jnp.floor((row_low + 0.5) * (1.0 / degree_one))
    weight = 8.0 / (
        (2.0 * row_high + 1.0) * (2.0 * mid + 1.0) * (2.0 * (row_low - degree_one * mid) + 1.0)
    )
    weight = jnp.concatenate([weight] * (width // LANES), axis=1)[:modes]

    def split(chunk):
        for var in range(nvar):
            high, low = halves(state_ref[var, :, chunk * width : (chunk + 1) * width])
            for place, part in ((0, high), (size, low)):
                right_ref[chunk % 2, place + var * LANES : place + var * LANES + modes] = part

    def multiply(chunk):
        product_ref[chunk % 2] = mxu(matrix_ref[:, : 2 * size], right_ref[chunk % 2]) + mxu(
            matrix_ref[:, 2 * size :], right_ref[chunk % 2, :size]
        )

    split(0)
    multiply(0)
    split(1)
    copies[2].wait()
    copies[3].wait()
    below = [jnp.zeros((face, LANES), F32)] * nvar
    for chunk in range(chunks):
        first = chunk * width
        lanes = slice(first, first + width)
        if chunk + 1 < chunks:
            multiply(chunk + 1)
        if chunk + 2 < chunks:
            split(chunk + 2)
        scale = weight * jac_ref[:, lanes]
        for var in range(nvar):
            upper, lower = trace_sums(state_ref, var, first, width)
            if chunk + 1 < chunks:
                above = trace_sums(state_ref, var, first + width, LANES)[1]
            else:
                above = jnp.zeros((face, LANES), F32)
            above = jnp.concatenate([lower[:, LANES:], above], axis=1)
            under = jnp.concatenate([below[var], upper[:, : width - LANES]], axis=1)
            below[var] = upper[:, width - LANES :]
            plus = penalty_ref[var] * (above + under)
            minus = penalty_ref[var] * (above - under)
            for i in range(degree_one):
                face_ref[var, i * face : (i + 1) * face] = minus if i % 2 else plus
            change = state_ref[var, :, lanes] - old_ref[var, :, lanes]
            out_ref[var, :, lanes] = (
                product_ref[chunk % 2, var * LANES : var * LANES + modes] + scale * change
            ) - face_ref[var, :modes]
    copies[4].wait()


def cut_kernel(
    owner_vmem, got_ref, mass_hbm, operator_hbm, out_ref, owner_ref, mass_ref, operator_ref, left_ref, term_ref,
    spot_ref, seen_ref, sems,
):
    groups, modes = mass_ref.shape[:2]
    peers, nvar = out_ref.shape[0], out_ref.shape[1]
    kinds = got_ref.shape[1]
    owner_copy = pltpu.make_async_copy(owner_vmem, owner_ref, sems.at[0, groups])
    owner_copy.start()
    copies = []
    for group in range(groups):
        rows = slice(group * SUBS, (group + 1) * SUBS)
        copies.append(
            (
                pltpu.make_async_copy(mass_hbm.at[:, rows], mass_ref.at[group], sems.at[0, group]),
                pltpu.make_async_copy(operator_hbm.at[:, rows], operator_ref.at[group], sems.at[1, group]),
            )
        )
        for copy in copies[-1]:
            copy.start()
    out_ref[...] = jnp.zeros_like(out_ref)
    for peer in range(peers):
        seen_ref[peer] = 0
    owner_copy.wait()
    got = got_ref.reshape(peers * kinds * SUBS, LANES)
    out = out_ref.reshape(peers * nvar * SUBS, LANES)
    for index in range(groups * SUBS):
        owner = owner_ref[index]
        place = seen_ref[owner]
        seen_ref[owner] = place + 1
        spot_ref[index] = owner * (nvar * SUBS) + place
        first = owner * (kinds * SUBS) + place
        states = got[pl.ds(first, nvar, stride=SUBS), :]
        changes = states - got[pl.ds(first + nvar * SUBS, nvar, stride=SUBS), :]
        for kind, value in enumerate((changes, -states)):
            lanes = slice(kind * LANES, (kind + 1) * LANES)
            high = value.astype(BF16).astype(F32)
            left_ref[index, :nvar, lanes] = high
            left_ref[index, SUBS : SUBS + nvar, lanes] = value - high
    zero = jnp.zeros((modes, LANES - modes), F32)
    for group in range(groups):
        for copy in copies[group]:
            copy.wait()
        for inner in range(SUBS):
            index = group * SUBS + inner
            blocks = []
            for ref in (mass_ref.at[group], operator_ref.at[group]):
                block = ref.reshape(modes * SUBS, modes)[pl.ds(inner, modes, stride=SUBS), :]
                blocks.append(jnp.concatenate([block, zero], axis=1))
            high, low = halves(jnp.concatenate(blocks, axis=1))
            left = left_ref[index].astype(BF16)
            total = mxu(left, high, NT) + mxu(left, low, NT)
            term_ref[index, :, :modes] = total[:SUBS] + total[SUBS:]
    for index in range(groups * SUBS):
        out[pl.ds(spot_ref[index], nvar, stride=SUBS), :modes] = term_ref[index, :nvar, :modes]


def body_kernel(
    bodies, count, share, got_ref, rows_hbm, column_hbm, base_ref, out_ref,
    rows_ref, column_ref, data_ref, basis_ref, lift_ref, left_ref, sems,
):
    peers = got_ref.shape[0]
    nvar, modes, elems = out_ref.shape
    degree_one = DEGREE + 1
    copies = [
        pltpu.make_async_copy(source, target, sems.at[index])
        for index, (source, target) in enumerate(
            ((rows_hbm, rows_ref), (column_hbm, column_ref))
        )
    ]
    for copy in copies:
        copy.start()
    for peer in range(peers):
        data_ref[peer * share : (peer + 1) * share] = got_ref[peer, 2 * nvar, 1 : 1 + share]
    lift_ref[...] = jnp.zeros_like(lift_ref)
    mode, degree = iota((LANES, SUBS), 0), iota((LANES, SUBS), 1)
    real = mode < modes
    spreads = []
    for digit in (mode // (degree_one * degree_one), mode // degree_one % degree_one, mode % degree_one):
        chosen = (real & (digit == degree)).astype(BF16)
        spreads.append(jnp.concatenate([chosen, chosen, chosen], axis=1))
    ones = jnp.ones((1, LANES), F32)
    none = jnp.zeros((SUBS - degree_one, LANES), F32)
    for body in range(bodies):
        basis = None
        for axis in range(3):
            coords = data_ref[body * 7 + axis : body * 7 + axis + 1]
            table = [ones, coords]
            for n in range(1, DEGREE):
                table.append(((2.0 * n + 1.0) * coords * table[n] - n * table[n - 1]) / (n + 1.0))
            stacked = jnp.concatenate(table + [none], axis=0)
            high = stacked.astype(BF16)
            middle, low = halves(stacked - high.astype(F32))
            factor = mxu(spreads[axis], jnp.concatenate([high, middle, low], axis=0))
            basis = factor if basis is None else basis * factor
        basis_ref[0, body], basis_ref[1, body] = halves(basis)
    bases = [(basis_ref[0, body], basis_ref[1, body]) for body in range(bodies)]
    traces = []
    copies[0].wait()
    for body in range(bodies):
        rows = jnp.concatenate([rows_ref[var, body * count : (body + 1) * count] for var in range(nvar)], axis=0)
        traces.append(product(halves(rows), bases[body]))
    fluxes = []
    for body in range(bodies):
        trace = [traces[body][var * count : (var + 1) * count] for var in range(nvar)]
        normal = [data_ref[body * 7 + 3 + axis : body * 7 + 4 + axis] for axis in range(3)]
        weights = data_ref[body * 7 + 6 : body * 7 + 7]
        speed = normal[0] * trace[1] + normal[1] * trace[2] + normal[2] * trace[3]
        flux = [speed + 0.5 * trace[0]] + [normal[axis] * trace[4] for axis in range(3)] + [1.4 * speed]
        fluxes.append(halves(jnp.concatenate([part * weights for part in flux], axis=0)))
    for body in range(bodies):
        lifted = product(fluxes[body], bases[body], NT)
        for var in range(nvar):
            lift_ref[var, body * count : (body + 1) * count] = lifted[var * count : (var + 1) * count]
    for var in range(nvar):
        high, low = halves(lift_ref[var].T)
        left_ref[var * LANES : (var + 1) * LANES, :LANES] = high
        left_ref[var * LANES : (var + 1) * LANES, LANES:] = low

    width = 2 * LANES
    copies[1].wait()
    spots = jnp.concatenate([column_ref[...]] * (width // LANES), axis=1)
    for first in range(0, elems, width):
        chosen = (spots == iota((LANES, width), 1) + first).astype(BF16)
        added = mxu(left_ref[...], jnp.concatenate([chosen, chosen], axis=0))
        for var in range(nvar):
            lanes = slice(first, first + width)
            out_ref[var, :, lanes] = base_ref[var, :, lanes] - added[var * LANES : var * LANES + modes]


def rim_kernel(penalty_ref, first_ref, second_ref, base_ref, out_ref, face_ref):
    nvar, modes, elems = out_ref.shape
    degree_one = DEGREE + 1
    face = modes // degree_one
    even = lax.axis_index("px") % 2 == 0
    bottom, top = slice(0, LANES), slice(elems - LANES, elems)
    for var in range(nvar):
        first, second = first_ref[var, :face], second_ref[var, :face]
        above = penalty_ref[var] * jnp.where(even, first, second)
        below = penalty_ref[var] * jnp.where(even, second, first)
        for i in range(degree_one):
            face_ref[0, var, i * face : (i + 1) * face] = -below if i % 2 else below
            face_ref[1, var, i * face : (i + 1) * face] = above
    for var in range(nvar):
        out_ref[var, :, bottom] = base_ref[var, :, bottom] - face_ref[0, var, :modes]
        out_ref[var, :, top] = base_ref[var, :, top] - face_ref[1, var, :modes]


def last_kernel(got_ref, column_ref, base_ref, out_hbm, out_ref, chosen_ref, sems):
    nvar, modes, elems = out_ref.shape
    slots = column_ref.shape[0]
    for layer in range(elems // LANES):
        lanes = slice(layer * LANES, (layer + 1) * LANES)
        chosen = (column_ref[...] == iota((slots, LANES), 1) + layer * LANES).astype(BF16)
        chosen_ref[:slots, lanes] = chosen
        chosen_ref[slots:, lanes] = chosen
    copies = []
    for var in range(nvar):
        left = jnp.concatenate(halves(got_ref[:, var].reshape(slots, LANES).T), axis=1)
        out_ref[var] = base_ref[var] + mxu(left, chosen_ref[...])[:modes]
        copies.append(pltpu.make_async_copy(out_ref.at[var], out_hbm.at[var], sems.at[var]))
        copies[-1].start()
    for copy in copies:
        copy.wait()


def swap(value, axis, odd):
    count = lax.axis_size(axis)
    pairs = [(low, low + 1) for low in range(odd, count - 1, 2)]
    return lax.ppermute(value, axis, pairs + [(high, low) for low, high in pairs])


def exchange(value):
    return lax.all_to_all(value, "py", split_axis=0, concat_axis=0, tiled=True)


def local(
    current_state, state_old, jacobian, volume_operator_list, flux_jacobian_list, penalty, cut_owner, cut_element,
    cut_mass, cut_operator, body_holder_index, body_points, body_normals, body_weights, covered,
):
    nvar, modes, elems = current_state.shape
    columns = elems // LAYERS
    face = modes // (DEGREE + 1)
    peers = lax.axis_size("py")
    cuts = cut_owner.shape[0]
    bodies, count = covered.shape
    cap = max(2, cuts * 3 // (2 * peers) + 1)
    share = -(-bodies * 7 // peers)
    half = LANES // 2
    slots = peers * SUBS
    assert columns == LANES and peers * cap <= half and bodies * count <= LANES
    assert cap <= SUBS and 1 + share <= SUBS and modes <= LANES and cuts % SUBS == 0
    shaped = jax.ShapeDtypeStruct
    wide = 2 * LANES
    size = nvar * LANES

    owner_row = in_hbm(cut_owner.reshape(1, cuts))
    small = [in_hbm(array) for array in (cut_element.reshape(1, cuts), body_points, body_normals, body_weights)]
    asked = shaped((peers, SUBS, LANES), F32)
    asked = pl.pallas_call(
        functools.partial(ids_kernel, cap, share),
        grid=(1,),
        out_shape=pltpu.VMEM(asked.shape, F32),
        in_specs=[scalars(), whole(owner_row)] + [whole(array) for array in small],
        out_specs=kept(),
        scratch_shapes=[pltpu.VMEM((pad8(peers * share), LANES), F32)],
        compiler_params=params(4),
        name="ids",
    )(in_hbm(body_holder_index), owner_row, *small)
    requests = exchange(asked)

    field = pltpu.VMEM(current_state.shape, F32)
    face_rows = shaped((nvar, pad8(face), LANES), F32)
    stack = shaped((nvar, LANES, LANES), F32)
    square = shaped((LANES, LANES), jnp.int32)
    scratch = pltpu.VMEM(stack.shape, F32)
    flux = in_hbm(flux_jacobian_list.transpose(1, 0, 2))
    state, first_rim, second_rim, covered_rows, covered_column, operator, flux, penalties = pl.pallas_call(
        load_kernel,
        grid=(1,),
        out_shape=(
            field,
            face_rows,
            stored(face_rows),
            stored(stack),
            stored(square),
            pltpu.VMEM(volume_operator_list.shape, F32),
            pltpu.VMEM(flux.shape, F32),
            pltpu.VMEM(penalty.shape, F32),
        ),
        in_specs=[remote()] * 5,
        out_specs=(kept(), whole(face_rows), whole(face_rows), whole(stack), whole(square)) + (kept(),) * 3,
        scratch_shapes=[
            pltpu.VMEM(covered.shape, jnp.int32),
            scratch,
            pltpu.SemaphoreType.DMA((nvar + 4,)),
        ],
        compiler_params=params(4),
        name="load",
    )(in_hbm(covered), in_hbm(current_state), in_hbm(volume_operator_list), flux, in_hbm(penalty))
    first_rim = swap(first_rim, "px", 0)

    reply = shaped((peers, 2 * nvar + 1, SUBS, LANES), F32)
    column = shaped((slots, LANES), jnp.int32)
    states_out, slot_column = pl.pallas_call(
        functools.partial(pick_kernel, cap),
        grid=(1,),
        out_shape=(stored(reply), pltpu.VMEM(column.shape, column.dtype)),
        in_specs=[kept(), kept(), remote()],
        out_specs=(remote(), kept()),
        scratch_shapes=[
            pltpu.VMEM(reply.shape, F32),
            pltpu.VMEM(current_state.shape, F32),
            scratch,
            pltpu.SemaphoreType.DMA((3 * nvar + 1,)),
        ],
        compiler_params=params(6),
        name="pick",
    )(requests, in_vmem(state), in_hbm(state_old))
    replies = exchange(states_out)

    jacobian_row = in_hbm(jacobian.reshape(1, elems))
    groups = cuts // SUBS
    mass_cols, operator_cols = in_hbm(cut_mass.transpose(1, 0, 2)), in_hbm(cut_operator.transpose(1, 0, 2))
    residual, owner_row, second_rim = pl.pallas_call(
        main_kernel,
        grid=(1,),
        out_shape=(field, pltpu.VMEM((cuts,), jnp.int32), stored(face_rows)),
        in_specs=[kept()] * 4 + [remote()] * 4,
        out_specs=(kept(), kept(), remote()),
        scratch_shapes=[
            pltpu.SMEM((nvar, 3, nvar), F32),
            pltpu.SMEM((nvar,), F32),
            pltpu.VMEM((1, elems), F32),
            pltpu.VMEM(current_state.shape, F32),
            pltpu.VMEM((3, LANES, LANES), F32),
            pltpu.VMEM((size, 3 * size), BF16),
            pltpu.VMEM((2, 2 * size, wide), BF16),
            pltpu.VMEM((2, size, wide), F32),
            pltpu.VMEM((nvar, LANES, wide), F32),
            pltpu.SemaphoreType.DMA((5,)),
        ],
        input_output_aliases={3: 0, 7: 2},
        compiler_params=params(20),
        cost_estimate=pl.CostEstimate(
            flops=6 * size * size * elems, transcendentals=0, bytes_accessed=4 * 4 * nvar * modes * elems
        ),
        name="main",
    )(
        in_vmem(flux), in_vmem(penalties), in_vmem(operator), in_vmem(state), jacobian_row, in_hbm(state_old),
        in_hbm(cut_owner.reshape(cuts)), in_hbm(second_rim),
    )
    second_rim = swap(second_rim, "px", 1)

    terms = shaped((peers, nvar, SUBS, LANES), F32)
    blocks = pltpu.VMEM((groups, modes, SUBS, modes), F32)
    results_out = pl.pallas_call(
        cut_kernel,
        grid=(1,),
        out_shape=pltpu.VMEM(terms.shape, F32),
        in_specs=[kept(), kept(), remote(), remote()],
        out_specs=kept(),
        scratch_shapes=[
            pltpu.SMEM((cuts,), jnp.int32),
            blocks,
            blocks,
            pltpu.VMEM((cuts, 2 * SUBS, 2 * LANES), F32),
            pltpu.VMEM((cuts, SUBS, LANES), F32),
            pltpu.SMEM((cuts,), jnp.int32),
            pltpu.SMEM((peers,), jnp.int32),
            pltpu.SemaphoreType.DMA((2, groups + 1)),
        ],
        compiler_params=params(10),
        name="cut",
    )(
        in_vmem(owner_row), replies, mass_cols, operator_cols,
    )
    results = exchange(results_out)

    residual = pl.pallas_call(
        functools.partial(body_kernel, bodies, count, share),
        grid=(1,),
        out_shape=field,
        in_specs=[kept(), remote(), remote(), kept()],
        out_specs=kept(),
        scratch_shapes=[
            scratch,
            pltpu.VMEM(square.shape, jnp.int32),
            pltpu.VMEM((pad8(peers * share), LANES), F32),
            pltpu.VMEM((2, bodies, LANES, LANES), BF16),
            scratch,
            pltpu.VMEM((size, wide), BF16),
            pltpu.SemaphoreType.DMA((2,)),
        ],
        input_output_aliases={3: 0},
        compiler_params=params(6),
        name="body",
    )(replies, in_hbm(covered_rows), in_hbm(covered_column), in_vmem(residual))

    residual = pl.pallas_call(
        rim_kernel,
        grid=(1,),
        out_shape=field,
        in_specs=[scalars()] + [kept()] * 3,
        out_specs=kept(),
        scratch_shapes=[pltpu.VMEM((2, nvar, LANES, LANES), F32)],
        input_output_aliases={3: 0},
        compiler_params=params(2),
        name="rim",
    )(in_hbm(penalty), first_rim, second_rim, in_vmem(residual))

    return pl.pallas_call(
        last_kernel,
        grid=(1,),
        out_shape=shaped(current_state.shape, F32),
        in_specs=[kept(), kept(), kept()],
        out_specs=remote(),
        scratch_shapes=[
            pltpu.VMEM(current_state.shape, F32),
            pltpu.VMEM((2 * slots, elems), BF16),
            pltpu.SemaphoreType.DMA((nvar,)),
        ],
        compiler_params=params(8),
        name="last",
    )(results, in_vmem(slot_column), in_vmem(residual))


def solution(mesh):
    both = ("px", "py")
    in_specs = (
        P(None, None, both),
        P(None, None, both),
        P(both),
        P(),
        P(),
        P(),
        P(both, None),
        P(both),
        P(both, None, None),
        P(both, None, None),
        P("px"),
        P(both, None, None),
        P(both, None, None),
        P(both, None),
        P(both, None),
    )

    return jax.shard_map(local, mesh=mesh, in_specs=in_specs, out_specs=P(None, None, both), check_vma=False)
```
